32 devices in a mesh: grp: 2 (over x), ra: 16 (over z, y, core).
Axes of the slice: x: 2, y: 2, z: 4, core: 2. Of those that a mesh axis runs over, the one named last changes fastest.
Arguments:
- pixels: bfloat16 [1536, 168, 168], P(('grp', 'ra')), parts along dimension 0, may hold values from -6 to 6
- inverse_var: bfloat16 [1536, 128, 128], P(('grp', 'ra')), parts along dimension 0, may hold values from 0.5 to 8
- psf_taps: bfloat16 [1536, 2, 41], P(('grp', 'ra')), parts along dimension 0, may hold values from -1 to 1
- warp_table: bfloat16 [64, 128, 128], replicated, may hold values from -1 to 1
- warp_index: int32 [1536, 2], P(('grp', 'ra')), parts along dimension 0, may hold values from 0 to 63
- dest_patch: int32 [1536, 1], P(('grp', 'ra')), parts along dimension 0, may hold values from 0 to 15; in each aligned block of 48 rows (0 to 47, 48 to 95, ...) at most 3 rows name the same one
- tile_row: int32 [1536], P(('grp', 'ra')), parts along dimension 0, may hold values from 0 to 3
- tile_col: int32 [1536], P(('grp', 'ra')), parts along dimension 0, may hold values from 0 to 4
Outputs:
- coadd: float32 [1024, 8192], P('grp', 'ra'), parts along dimension 0
- weight_map: float32 [1024, 8192], P('grp', 'ra'), parts along dimension 0
The draws below stay inside these ranges and needn't reach their ends.
There are 2 independent parts, one for each index of `grp`. The reference program is written for one: setup_inputs(seed, part) draws one part's arguments, and reference() takes and returns one part's arrays. A program takes and returns all parts, laid end to end along the dimension named above; an argument that names none is the same for every part. Nothing has to cross between parts.
Inputs may be any that keep to these rules, and one draw needn't show every extreme that they name: `dest_patch`: among the blocks of one device no patch is named more than 3 times; some device names some patch exactly 3 times.
All inputs are finite; a program needn't handle non-finite values.
Results may differ from the reference program's by a relative error of at most 0.0066.
Values may be sent and summed in bfloat16 or wider, within the bound.
No kernel may reach another device: no remote copies, remote signals or barrier semaphores. Data moves between devices by JAX's collectives and lax.ppermute only.
A program may use at most 128 MiB of HBM per device.

```python
import math
import jax
import jax.numpy as jnp
import numpy as np
from jax import lax

PIX = 128
TAPS = 41
TABLE = 64
TR = 4
TC = 4
BLK_DEV = 48
WIDE = 168
OWNERS = 16
CAP = 3
BLOCKS = 768


def lanczos(value):
    inside = jnp.abs(value) < 3.0
    return jnp.where(inside, jnp.sinc(value) * jnp.sinc(value / 3.0), 0.0)


def draw_warp_table(key, part):
    scale_key, shift_key, jitter_key = jax.random.split(key, 3)
    scales = jax.random.uniform(scale_key, (TABLE, 1, 1), jnp.float32, 0.97, 1.03)
    shifts = jax.random.uniform(shift_key, (TABLE, 1, 1), jnp.float32, 0.25, 0.75)
    jitter = jax.random.uniform(jitter_key, (TABLE, PIX, 1), jnp.float32, -0.1, 0.1)
    centre = (PIX - 1) / 2.0
    rows = jnp.arange(PIX, dtype=jnp.float32)[None, :, None]
    columns = jnp.arange(PIX, dtype=jnp.float32)[None, None, :]
    source = (rows - centre) * scales + centre + shifts + jitter
    return lanczos(columns - source).astype(jnp.bfloat16)


def touch_ends(values, stream_key, least, high):
    index_at = [jax.random.randint(jax.random.fold_in(stream_key, axis), (), 0, length) for axis, length in enumerate(values.shape)]
    longest = values.shape.index(max(values.shape))
    next_to = index_at[:longest] + [(index_at[longest] + 1) % values.shape[longest]] + index_at[longest + 1:]
    return values.at[tuple(index_at)].set(least).at[tuple(next_to)].set(high)


def steps_of(rng, extent, shards, least, high):
    factor_of, own = 1.0, jax.random.fold_in(rng, 6)
    for dim, blocks in shards:
        draws = jnp.exp(jax.random.uniform(jax.random.fold_in(own, dim), (blocks,), jnp.float32, least / len(shards), high / len(shards)))
        factor_of = factor_of * jnp.repeat(draws, extent[dim] // blocks).reshape([-1 if axis == dim else 1 for axis in range(len(extent))])
    return factor_of


def deal_out(rng, own, number, rows, amount, top, bound, slope):
    order = jax.random.permutation(rng, amount)
    heavy_load, usual = load_shares(amount, rows * top, bound, slope, True), load_shares(amount, rows * top, bound, slope, False)
    places = jnp.arange(amount)

    def named(lengths, turn):
        used = int((lengths > 0).sum())
        fixed = max(1, used // 4)
        passed = fixed + (places - fixed + turn * (used - fixed)) % max(1, amount - fixed)
        return jnp.zeros((amount,), jnp.int32).at[order[jnp.where(places < fixed, places, passed)]].set(jnp.asarray(lengths, jnp.int32))

    lengths = jnp.where(number % 4 == 0, named(heavy_load, number // 4), named(usual, number - number // 4 - 1))
    mixed = jax.random.permutation(jax.random.fold_in(own, 3), amount)
    giver, sink = mixed[0:amount // 2 * 2:2], mixed[1:amount // 2 * 2:2]
    margin = jnp.minimum(lengths[giver] - 1, bound - lengths[sink]) // 2
    margin = jnp.where((giver == order[0]) | (sink == order[0]) | (lengths[sink] == 0), 0, jnp.maximum(margin, 0))
    passed = jax.random.randint(jax.random.fold_in(own, 4), (amount // 2,), 0, 1 << 20) % (margin + 1)
    lengths = lengths.at[giver].add(-passed).at[sink].add(passed)
    labels = jnp.searchsorted(jnp.cumsum(lengths), jnp.arange(rows * top), side="right").astype(jnp.int32)
    table = labels.reshape(top, rows).T
    table = table[jax.random.permutation(jax.random.fold_in(own, 1), rows)]
    turn = jax.random.randint(jax.random.fold_in(own, 2), (rows, 1), 0, top)
    return jnp.take_along_axis(table, (jnp.arange(top)[None, :] + turn) % top, axis=1)


def load_shares(amount, total, reach, lean, full):
    portions = [(1 << 20) // math.isqrt(rank ** lean) + 1 for rank in range(1, amount + 1)]
    largest = reach if full else min(reach, max(-(-total // amount), total * portions[0] // sum(portions)))
    least = 1 if total - largest >= amount - 1 else 0
    holding, rest = [largest] + [least] * (amount - 1), total - largest - least * (amount - 1)
    while rest > 0:
        movable = [i for i in range(1, amount) if holding[i] < largest] or [i for i in range(1, amount) if holding[i] < reach]
        mass, left = sum([portions[i] for i in movable]), rest
        for i in movable:
            extra = min(reach - holding[i], max(1, left * portions[i] // mass), rest)
            holding[i] = holding[i] + extra
            rest = rest - extra
    return np.array(holding)


def normal_values(key, shape, scale, limit, cuts=(), kind=jnp.bfloat16):
    entries = scale * jax.random.normal(key, shape, jnp.float32)
    if cuts:
        entries = entries * steps_of(key, shape, cuts, -0.22, 0.18)
    return jnp.clip(entries, -limit, limit).astype(kind)


def setup_inputs(seed: int = 0, part: int = 0) -> dict:
    seeds = jax.random.split(jax.random.key(seed), 9)
    part_splits = jax.random.split(jax.random.fold_in(seeds[8], part), 9)
    pixels = normal_values(part_splits[0], (BLOCKS, WIDE, WIDE), 1.0, 6.0, ((0, 16),))
    inverse_var = jnp.clip(jnp.exp(math.log(8.0) - 2.7725887 * jax.random.uniform(part_splits[1], (BLOCKS, PIX, PIX), jnp.float32) ** steps_of(part_splits[1], (BLOCKS, PIX, PIX), ((0, 16),), -0.2, 0.2)), 0.5, 8.0).astype(jnp.bfloat16)
    psf_taps = normal_values(part_splits[2], (BLOCKS, 2, TAPS), TAPS ** -0.5, 1.0, ((0, 16),))
    warp_table = draw_warp_table(jax.random.fold_in(seeds[8], 71), part)
    warp_index = touch_ends(jax.random.randint(part_splits[4], (BLOCKS, 2), 0, TABLE), jax.random.fold_in(part_splits[4], 1), 0, TABLE - 1).astype(jnp.int32)
    dest_patch_keys = jax.random.split(jax.random.fold_in(part_splits[5], 1), BLOCKS // BLK_DEV)
    dest_patch_turns = jax.random.permutation(jax.random.fold_in(part_splits[5], 3), BLOCKS // BLK_DEV)
    dest_patch = jax.vmap(lambda own, number: deal_out(jax.random.fold_in(part_splits[5], 2), own, number, BLK_DEV, OWNERS, 1, CAP, 2))(dest_patch_keys, dest_patch_turns).reshape((BLOCKS, 1))
    tile_row = touch_ends(jax.random.randint(part_splits[6], (BLOCKS,), 0, TR), jax.random.fold_in(part_splits[6], 1), 0, TR - 1).astype(jnp.int32)
    tile_col = touch_ends(jax.random.randint(part_splits[7], (BLOCKS,), 0, TC + 1), jax.random.fold_in(part_splits[7], 1), 0, TC).astype(jnp.int32)
    return dict(pixels=pixels, inverse_var=inverse_var, psf_taps=psf_taps, warp_table=warp_table, warp_index=warp_index, dest_patch=dest_patch, tile_row=tile_row, tile_col=tile_col)


def toeplitz(tap_values):
    offset_grid = jnp.arange(WIDE, dtype=jnp.int32)[None, :] - jnp.arange(PIX, dtype=jnp.int32)[:, None]
    inside = (offset_grid >= 0) & (offset_grid < TAPS)
    picked = tap_values[jnp.clip(offset_grid, 0, TAPS - 1).astype(jnp.int32)]
    return jnp.where(inside, picked, jnp.zeros_like(picked))


def reference(pixels, inverse_var, psf_taps, warp_table, warp_index, dest_patch, tile_row, tile_col):
    cycle = OWNERS * TC
    tile_count = TR * cycle
    f32 = jnp.float32
    bf16 = jnp.bfloat16

    def one_device(running, device_data):
        pix_dev, ivar_dev, taps_dev, widx_dev, dest_dev, row_dev, col_dev = device_data
        row_kernel = jax.vmap(toeplitz)(taps_dev[:, 0]).astype(f32)
        col_kernel = jax.vmap(toeplitz)(taps_dev[:, 1]).astype(f32)
        col_pass = jnp.einsum('bij,bkj->bik', pix_dev.astype(f32), col_kernel).astype(bf16)
        matched = jnp.einsum('bij,bjk->bik', row_kernel, col_pass.astype(f32))
        weighted = (matched * ivar_dev.astype(f32)).astype(bf16)
        stacked = jnp.stack([weighted, ivar_dev], 1).astype(f32)
        warp_rows = warp_table[widx_dev[:, 0]].astype(f32)
        warp_cols = warp_table[widx_dev[:, 1]].astype(f32)
        middle = jnp.einsum('bij,bsjk->bsik', warp_rows, stacked).astype(bf16)
        warped = jnp.einsum('bsij,bkj->bsik', middle.astype(f32), warp_cols).astype(bf16)
        global_col = (dest_dev[:, 0] * TC + col_dev) % cycle
        tile_index = (row_dev * cycle + global_col).astype(jnp.int32)
        added = jax.ops.segment_sum(warped.astype(f32), tile_index, num_segments=tile_count)
        return running + added, None

    def split(array):
        return array.reshape((OWNERS, BLK_DEV) + array.shape[1:])

    start = jnp.zeros((tile_count, 2, PIX, PIX), f32)
    totals, unused = lax.scan(one_device, start, (split(pixels), split(inverse_var), split(psf_taps), split(warp_index), split(dest_patch), split(tile_row), split(tile_col)))
    totals = totals.reshape(TR, cycle, 2, PIX, PIX)
    numerator = totals[:, :, 0].transpose(0, 2, 1, 3).reshape(TR * PIX, cycle * PIX)
    weight_map = totals[:, :, 1].transpose(0, 2, 1, 3).reshape(TR * PIX, cycle * PIX)
    coadd = numerator / jnp.maximum(weight_map, 1.0)
    return coadd, weight_map
```

```python
import functools

import jax
import jax.numpy as jnp
from jax import lax
from jax.experimental import pallas as pl
from jax.experimental.pallas import tpu as pltpu
from jax.sharding import PartitionSpec as P

TR = 4
TC = 4
TILES = TR * (TC + 1)
LAST = 4

SMEM = pl.BlockSpec(memory_space=pltpu.SMEM)
VMEM = pl.BlockSpec(memory_space=pltpu.VMEM)


def dot(left, right):
    return jnp.dot(left, right, preferred_element_type=jnp.float32).astype(jnp.bfloat16)


def dot_t(left, right):
    return lax.dot_general(
        left, right, (((1,), (1,)), ((), ())), preferred_element_type=jnp.float32
    )


def slots_body(owners, capacity, dest, row, col, order, ids):
    blocks = dest.shape[0]
    me = lax.axis_index("ra")

    def clear(slot, carry):
        order[slot] = 0
        ids[slot] = TILES
        return carry

    lax.fori_loop(0, owners * capacity, clear, 0)

    def counting(count):
        def zero(owner, carry):
            count[owner] = 0
            return carry

        lax.fori_loop(0, owners, zero, 0)

        def place(block, carry):
            owner = dest[block]
            rank = count[owner]
            count[owner] = rank + 1
            order[(owner ^ me) * capacity + rank] = block
            ids[owner * capacity + rank] = row[block] * (TC + 1) + col[block]
            return carry

        lax.fori_loop(0, blocks, place, 0)

    pl.run_scoped(counting, pltpu.SMEM((owners,), jnp.int32))


def warp_den(order, widx, ivar, table, outs, steps, capacity):
    for step, out in zip(steps, outs):
        for rank in range(capacity):
            block = order[step * capacity + rank]
            middle = dot(table[widx[0, block]], ivar[block])
            out[rank] = dot_t(middle, table[widx[1, block]]).astype(jnp.bfloat16)


def den_first_kernel(owners, capacity, steps, dest, row, col, widx, ivar, table, order, ids, *outs):
    slots_body(owners, capacity, dest, row, col, order, ids)
    warp_den(order, widx, ivar, table, outs, steps, capacity)


def den_kernel(capacity, steps, order, widx, ivar, table, *outs):
    warp_den(order, widx, ivar, table, outs, steps, capacity)


def toeplitz(taps, side, wide):
    lanes = lax.broadcasted_iota(jnp.int32, (8, 128), 1)
    base = pltpu.roll(jnp.broadcast_to(taps, (8, 128)), 0, 1, stride=1, stride_axis=0)
    ntaps = wide - side + 1
    low, high = [], []
    for start in range(0, side, 8):
        turned = pltpu.roll(base, start, 1) if start else base
        if start + 7 + ntaps <= 128:
            low.append(turned)
            high.append(jnp.zeros_like(turned))
        else:
            low.append(jnp.where(lanes >= 64, turned, 0.0))
            high.append(jnp.where(lanes >= 64, 0.0, turned))
    both = jnp.concatenate([jnp.concatenate(low, 0), jnp.concatenate(high, 0)], 1)
    return both.astype(jnp.bfloat16)[:, :wide]


def num_kernel(capacity, steps, order, widx, pixels, ivar, taps, table, *outs):
    side, wide = ivar.shape[1], pixels.shape[1]
    for step, out in zip(steps, outs):
        for rank in range(capacity):
            block = order[step * capacity + rank]
            rows = toeplitz(taps[block, 0:1, :], side, wide)
            cols = toeplitz(taps[block, 1:2, :], side, wide)
            colpass = dot_t(pixels[block], cols).astype(jnp.bfloat16)
            matched = jnp.dot(rows, colpass, preferred_element_type=jnp.float32)
            weighted = (matched * ivar[block].astype(jnp.float32)).astype(jnp.bfloat16)
            middle = dot(table[widx[0, block]], weighted)
            out[rank] = dot_t(middle, table[widx[1, block]]).astype(jnp.bfloat16)


def sum_kernel(capacity, steps, has_total, last, ids, *refs):
    me = lax.axis_index("ra")
    arrived = refs[: len(steps)]
    refs = refs[len(steps) :]
    if has_total:
        before, refs = refs[0], refs[1:]
    total = refs[0]
    total[...] = before[...] if has_total else jnp.zeros_like(total)
    for step, blocks in zip(steps, arrived):
        for rank in range(capacity):
            tile = ids[(step ^ me) * capacity + rank]
            total[tile] = total[tile] + blocks[rank].astype(jnp.float32)
    if last:
        for row in range(TR):
            refs[1][row] = total[row * (TC + 1) + TC].astype(jnp.bfloat16)


def finish_kernel(num, den, num_in, den_in, coadd, weight_map):
    side = num.shape[1]
    for row in range(TR):
        for col in range(TC):
            n, d = num[row * (TC + 1) + col], den[row * (TC + 1) + col]
            if col == 0:
                n = n + num_in[row].astype(jnp.float32)
                d = d + den_in[row].astype(jnp.float32)
            at = (slice(row * side, (row + 1) * side), slice(col * side, (col + 1) * side))
            weight_map[at] = d
            coadd[at] = n / jnp.maximum(d, 1.0)


def exchanged(value, owners, step):
    if step == 0:
        return value
    return lax.ppermute(value, "ra", [(source, source ^ step) for source in range(owners)])


def passed_along(value, owners):
    return lax.ppermute(value, "ra", [(source, (source + 1) % owners) for source in range(owners)])


def shards(pixels, inverse_var, psf_taps, warp_table, warp_index, dest_patch, tile_row, tile_col):
    blocks = pixels.shape[0]
    side = inverse_var.shape[1]
    owners = lax.axis_size("ra")
    capacity = max(2, blocks // owners)
    half = owners // 2
    far, near = list(range(half, owners)), list(range(half))
    bf16, f32 = jnp.bfloat16, jnp.float32
    sent = jax.ShapeDtypeStruct((capacity, side, side), bf16)
    slots = jax.ShapeDtypeStruct((owners * capacity,), jnp.int32)
    totals = jax.ShapeDtypeStruct((TILES + 1, side, side), f32)
    border = jax.ShapeDtypeStruct((TR, side, side), bf16)

    widx = warp_index.T
    taps = jnp.pad(psf_taps.astype(f32), ((0, 0), (0, 0), (0, 128 - psf_taps.shape[2])))

    def cost(count, flops):
        return pl.CostEstimate(flops=count * flops, bytes_accessed=count * 65536, transcendentals=0)

    order, ids, *den_far = pl.pallas_call(
        functools.partial(den_first_kernel, owners, capacity, far),
        out_shape=[slots, slots] + [sent] * len(far),
        in_specs=[SMEM] * 4 + [VMEM] * 2,
        out_specs=[SMEM] * 2 + [VMEM] * len(far),
        cost_estimate=cost(len(far) * capacity, 8 << 20),
        name="den_far",
    )(dest_patch[:, 0], tile_row, tile_col, widx, inverse_var, warp_table)

    def den(steps, name):
        return pl.pallas_call(
            functools.partial(den_kernel, capacity, steps),
            out_shape=[sent] * len(steps),
            in_specs=[SMEM] * 2 + [VMEM] * 2,
            out_specs=[VMEM] * len(steps),
            cost_estimate=cost(len(steps) * capacity, 8 << 20),
            name=name,
        )(order, widx, inverse_var, warp_table)

    def num(steps, name):
        return pl.pallas_call(
            functools.partial(num_kernel, capacity, steps),
            out_shape=[sent] * len(steps),
            in_specs=[SMEM] * 2 + [VMEM] * 4,
            out_specs=[VMEM] * len(steps),
            cost_estimate=cost(len(steps) * capacity, 22 << 20),
            name=name,
        )(order, widx, pixels, inverse_var, taps, warp_table)

    den_all = dict(zip(far, den_far))
    num_all = dict(zip(far, num(far, "num_far")))
    den_all.update(zip(near, den(near, "den_near")))
    num_all.update(zip(near, num(near, "num_near")))
    ids_in = lax.all_to_all(
        ids.reshape(owners, capacity), "ra", split_axis=0, concat_axis=0, tiled=True
    ).reshape(-1)
    den_in = {step: exchanged(den_all[step], owners, step) for step in far}
    num_in = {step: exchanged(num_all[step], owners, step) for step in far}
    den_in.update({step: exchanged(den_all[step], owners, step) for step in near})
    num_in.update({step: exchanged(num_all[step], owners, step) for step in near})

    def summed(arrived, steps, before, last, name):
        given = [arrived[step] for step in steps] + ([] if before is None else [before])
        return pl.pallas_call(
            functools.partial(sum_kernel, capacity, steps, before is not None, last),
            out_shape=[totals, border] if last else [totals],
            in_specs=[SMEM] + [VMEM] * len(given),
            out_specs=[VMEM, VMEM] if last else [VMEM],
            cost_estimate=cost(len(steps) * capacity, 1 << 15),
            name=name,
        )(ids_in, *given)

    den_total, den_border = summed(den_in, near + far, None, True, "den_sum")
    den_border = passed_along(den_border, owners)
    (num_part,) = summed(num_in, near + far[:-LAST], None, False, "num_sum_early")
    num_total, num_border = summed(num_in, far[-LAST:], num_part, True, "num_sum_late")
    num_border = passed_along(num_border, owners)
    sky = jax.ShapeDtypeStruct((TR * side, TC * side), f32)
    return tuple(
        pl.pallas_call(
            finish_kernel,
            out_shape=[sky, sky],
            in_specs=[VMEM] * 4,
            out_specs=[VMEM] * 2,
            name="finish",
        )(num_total, den_total, num_border, den_border)
    )


def solution(mesh):
    placed = (
        P(("grp", "ra"), None, None),
        P(("grp", "ra"), None, None),
        P(("grp", "ra"), None, None),
        P(),
        P(("grp", "ra"), None),
        P(("grp", "ra"), None),
        P(("grp", "ra")),
        P(("grp", "ra")),
    )
    return jax.shard_map(
        shards,
        mesh=mesh,
        in_specs=placed,
        out_specs=(P("grp", "ra"), P("grp", "ra")),
        check_vma=False,
    )
```

```python
import functools

import jax
import jax.numpy as jnp
from jax import lax
from jax.experimental import pallas as pl
from jax.experimental.pallas import tpu as pltpu
from jax.sharding import PartitionSpec as P

TR = 4
TC = 4
TILES = TR * (TC + 1)
IDS = 16
LATE = 2

SMEM = pl.BlockSpec(memory_space=pltpu.SMEM)
VMEM = pl.BlockSpec(memory_space=pltpu.VMEM)
ANY = pl.BlockSpec(memory_space=pl.ANY)


def dot(left, right):
    return jnp.dot(left, right, preferred_element_type=jnp.float32)


def dot_t(left, right):
    return lax.dot_general(
        left, right, (((1,), (1,)), ((), ())), preferred_element_type=jnp.float32
    )


def lanes():
    return lax.broadcasted_iota(jnp.int32, (8, 128), 1)


def staggered(row):
    return pltpu.roll(jnp.broadcast_to(row, (8, 128)), 0, 1, stride=1, stride_axis=0)


def row_kernel(taps, side, wide):
    base, ntaps = staggered(taps), wide - side + 1
    low, high = [], []
    for start in range(0, side, 8):
        turned = pltpu.roll(base, start, 1) if start else base
        if start + 7 + ntaps <= 128:
            low.append(turned)
            high.append(jnp.zeros_like(turned))
        else:
            low.append(jnp.where(lanes() >= 64, turned, 0.0))
            high.append(jnp.where(lanes() >= 64, 0.0, turned))
    both = jnp.concatenate([jnp.concatenate(low, 0), jnp.concatenate(high, 0)], 1)
    return both.astype(jnp.bfloat16)[:, :wide]


def col_kernel(backward, side, wide):
    base, ntaps = staggered(backward), wide - side + 1
    parts = []
    for start in range(0, wide, 8):
        at = start - (ntaps - 1)
        turned = pltpu.roll(base, at % 128, 1) if at % 128 else base
        if at < 0:
            turned = jnp.where(lanes() < 64, turned, 0.0)
        if at + 7 + ntaps > 128:
            turned = jnp.where(lanes() >= 64, turned, 0.0)
        parts.append(turned)
    return jnp.concatenate(parts, 0).astype(jnp.bfloat16)


def slots_body(owners, capacity, count, dest, row, col, order, ids):
    me = lax.axis_index("ra")

    def clear(slot, carry):
        order[slot] = 0
        ids[slot] = TILES
        return carry

    lax.fori_loop(0, owners * capacity, clear, 0)

    def zero(owner, carry):
        count[owner] = 0
        return carry

    lax.fori_loop(0, owners, zero, 0)

    def place(block, carry):
        owner = dest[block]
        rank = count[owner]
        count[owner] = rank + 1
        slot = (owner ^ me) * capacity + rank
        order[slot] = block
        ids[slot] = row[block] * (TC + 1) + col[block]
        return carry

    lax.fori_loop(0, dest.shape[0], place, 0)


def blocks_body(capacity, steps, order, ids, widx, arrays, outs, buffers, sem):
    pixels, ivar, taps, table = arrays
    px, iv, tp, rt, ct = buffers
    side, wide = ivar.shape[1], pixels.shape[1]
    copies = []
    for index, step in enumerate(steps):
        for rank in range(capacity):
            at = index * capacity + rank
            block = order[step * capacity + rank]
            pairs = (
                (taps.at[block], tp.at[at]),
                (pixels.at[block], px.at[at]),
                (ivar.at[block], iv.at[at]),
                (table.at[widx[0, block]], rt.at[at]),
                (table.at[widx[1, block]], ct.at[at]),
            )
            for kind, (source, target) in enumerate(pairs):
                copy = pltpu.make_async_copy(source, target, sem.at[kind, at])
                copy.start()
                copies.append(copy)
    for index, (step, out) in enumerate(zip(steps, outs)):
        at = range(index * capacity, (index + 1) * capacity)
        for copy in copies[5 * at[0] : 5 * (at[-1] + 1)]:
            copy.wait()
        cols = [col_kernel(tp[i, 1:2, :], side, wide) for i in at]
        rows = [row_kernel(tp[i, 0:1, :], side, wide) for i in at]
        passed = [dot(px[i], k).astype(jnp.bfloat16) for i, k in zip(at, cols)]
        weighted = [
            (dot(k, p) * iv[i].astype(jnp.float32)).astype(jnp.bfloat16)
            for i, k, p in zip(at, rows, passed)
        ]
        middle = [
            dot(rt[i], jnp.concatenate([w, iv[i]], 1)).astype(jnp.bfloat16)
            for i, w in zip(at, weighted)
        ]
        for rank, (i, m) in enumerate(zip(at, middle)):
            both = jnp.concatenate([m[:, :side], m[:, side:]], 0)
            out[pl.ds(rank * 2 * side, 2 * side), :] = dot_t(both, ct[i]).astype(jnp.bfloat16)
        which = lax.broadcasted_iota(jnp.int32, (IDS, side), 0)
        tiles = jnp.full((IDS, side), TILES, jnp.int32)
        for rank in range(capacity):
            tiles = jnp.where(which == rank, ids[step * capacity + rank], tiles)
        out[pl.ds(capacity * 2 * side, IDS), :] = tiles.astype(jnp.float32).astype(jnp.bfloat16)


def first_kernel(owners, capacity, steps, *refs):
    dest, row, col, widx = refs[:4]
    arrays, refs = refs[4:8], refs[8:]
    order, ids = refs[:2]
    outs, refs = refs[2 : 2 + len(steps)], refs[2 + len(steps) :]
    slots_body(owners, capacity, refs[-1], dest, row, col, order, ids)
    blocks_body(capacity, steps, order, ids, widx, arrays, outs, refs[:5], refs[5])


def next_kernel(capacity, steps, *refs):
    order, ids, widx = refs[:3]
    arrays, refs = refs[3:7], refs[8:]
    outs, refs = refs[: len(steps)], refs[len(steps) :]
    blocks_body(capacity, steps, order, ids, widx, arrays, outs, refs[:5], refs[5])


def fetched(sources, targets, sem):
    copies = []
    for index, (source, target) in enumerate(zip(sources, targets)):
        copy = pltpu.make_async_copy(source, target, sem.at[index])
        copy.start()
        copies.append(copy)
    return copies


def add_parcel(parcel, capacity, side, add):
    for rank in range(capacity):
        tile = parcel[pl.ds(capacity * 2 * side, IDS), :].astype(jnp.float32)[rank : rank + 1]
        add(jnp.max(tile).astype(jnp.int32), parcel.at[pl.ds(rank * 2 * side, 2 * side), :])


def early_kernel(capacity, count, *refs):
    parcels, (total, buffer, sem) = refs[:count], refs[count:]
    side = total.shape[2]
    copies = fetched(parcels, [buffer.at[i] for i in range(count)], sem)
    total[...] = jnp.zeros_like(total)

    def add(tile, block):
        total[tile] = total[tile] + block[...].astype(jnp.float32)

    for index, copy in enumerate(copies):
        copy.wait()
        add_parcel(buffer.at[index], capacity, side, add)


def border_kernel(capacity, count, total, *refs):
    parcels, (border, sums, buffer, sem) = refs[:count], refs[count:]
    side = border.shape[2]
    columns = [total.at[row * (TC + 1) + TC] for row in range(TR)]
    targets = [sums.at[row] for row in range(TR)] + [buffer.at[i] for i in range(count)]
    for copy in fetched(columns + list(parcels), targets, sem):
        copy.wait()

    def add(tile, block):
        row = lax.select(lax.rem(tile, TC + 1) == TC, lax.div(tile, TC + 1), TR)
        sums[row] = sums[row] + block[...].astype(jnp.float32)

    sums[TR] = jnp.zeros_like(sums[TR])
    for index in range(count):
        add_parcel(buffer.at[index], capacity, side, add)
    for row in range(TR):
        border[row] = sums[row].astype(jnp.bfloat16)


def spots(row, col, side):
    return pl.ds(row * side, side), pl.ds(col * side, side)


def inner_kernel(capacity, count, total, *refs):
    parcels, (coadd, weight_map, edge, sums, buffer, sem) = refs[:count], refs[count:]
    side = edge.shape[2]
    targets = [sums] + [buffer.at[i] for i in range(count)]
    for copy in fetched([total] + list(parcels), targets, sem):
        copy.wait()

    def add(tile, block):
        sums[tile] = sums[tile] + block[...].astype(jnp.float32)

    for index in range(count):
        add_parcel(buffer.at[index], capacity, side, add)
    for row in range(TR):
        edge[row] = sums[row * (TC + 1)]
        for col in range(TC):
            both = sums[row * (TC + 1) + col]
            num, den = both[:side], both[side:]
            weight_map[spots(row, col, side)] = den
            coadd[spots(row, col, side)] = num / jnp.maximum(den, 1.0)


def edge_kernel(edge, border, coadd_in, map_in, coadd, weight_map, num, den, sem):
    side = edge.shape[2]
    copies = []
    for row in range(TR):
        both = edge[row] + border[row].astype(jnp.float32)
        num[row] = both[:side] / jnp.maximum(both[side:], 1.0)
        den[row] = both[side:]
        for kind, (source, target) in enumerate(((num, coadd), (den, weight_map))):
            copy = pltpu.make_async_copy(
                source.at[row], target.at[spots(row, 0, side)], sem.at[kind, row]
            )
            copy.start()
            copies.append(copy)
    for copy in copies:
        copy.wait()


def exchanged(value, owners, step):
    if step == 0:
        return value
    return lax.ppermute(value, "ra", [(source, source ^ step) for source in range(owners)])


def passed_along(value, owners):
    return lax.ppermute(value, "ra", [(source, (source + 1) % owners) for source in range(owners)])


def planned(owners):
    half = owners // 2
    far = list(range(owners - 1, half - 1, -1))
    near = list(range(half - 1, -1, -1))
    cut = len(far) // 2
    steps = far[:cut] + near[: half // 2] + far[cut:] + near[half // 2 :]
    groups = [steps[:1]]
    for start in range(1, owners, 3):
        groups.append(steps[start : start + 3])
    return groups, far


def shards(pixels, inverse_var, psf_taps, warp_table, warp_index, dest_patch, tile_row, tile_col):
    blocks, wide = pixels.shape[:2]
    side = inverse_var.shape[1]
    owners = lax.axis_size("ra")
    capacity = max(2, blocks // owners)
    bf16, f32 = jnp.bfloat16, jnp.float32
    parcel = jax.ShapeDtypeStruct((capacity * 2 * side + IDS, side), bf16)
    slots = jax.ShapeDtypeStruct((owners * capacity,), jnp.int32)
    totals = (TILES + 1, 2 * side, side)

    def cost(count, flops, moved):
        return pl.CostEstimate(flops=count * flops, bytes_accessed=count * moved, transcendentals=0)

    widx = warp_index.T
    taps = jnp.stack([psf_taps[:, 0], psf_taps[:, 1, ::-1]], 1).astype(f32)
    taps = jnp.pad(taps, ((0, 0), (0, 6), (0, 128 - taps.shape[2])))
    arrays = (pixels, inverse_var, taps, warp_table)
    groups, far = planned(owners)

    def buffers(count):
        return [
            pltpu.VMEM((count, wide, wide), bf16),
            pltpu.VMEM((count, side, side), bf16),
            pltpu.VMEM((count, 8, 128), f32),
            pltpu.VMEM((count, side, side), bf16),
            pltpu.VMEM((count, side, side), bf16),
            pltpu.SemaphoreType.DMA((5, count)),
        ]

    sent = {}
    before = None
    for index, steps in enumerate(groups):
        count = len(steps) * capacity
        shared = dict(
            scratch_shapes=buffers(count),
            cost_estimate=cost(count, 30 << 20, 1 << 18),
            name="blocks_" + str(index),
        )
        if index == 0:
            shared["scratch_shapes"].append(pltpu.SMEM((owners,), jnp.int32))
            order, ids, *outs = pl.pallas_call(
                functools.partial(first_kernel, owners, capacity, steps),
                out_shape=[slots, slots] + [parcel] * len(steps),
                in_specs=[SMEM] * 4 + [ANY] * 4,
                out_specs=[SMEM] * 2 + [VMEM] * len(steps),
                **shared,
            )(dest_patch[:, 0], tile_row, tile_col, widx, *arrays)
        else:
            outs = pl.pallas_call(
                functools.partial(next_kernel, capacity, steps),
                out_shape=[parcel] * len(steps),
                in_specs=[SMEM] * 3 + [ANY] * 5,
                out_specs=[VMEM] * len(steps),
                **shared,
            )(order, ids, widx, *arrays, before)
        before = outs[0]
        sent.update(zip(steps, outs))
    steps = [step for group in groups for step in group]
    arrived = {step: exchanged(sent[step], owners, step) for step in steps}
    late = far[-LATE:]
    early = [step for step in steps if step not in late]

    def held(count):
        return [pltpu.VMEM((count,) + parcel.shape, bf16)]

    total = pl.pallas_call(
        functools.partial(early_kernel, capacity, len(early)),
        out_shape=jax.ShapeDtypeStruct(totals, f32),
        in_specs=[ANY] * len(early),
        out_specs=VMEM,
        scratch_shapes=held(len(early)) + [pltpu.SemaphoreType.DMA((len(early),))],
        cost_estimate=cost(len(early) * capacity, 1 << 16, 1 << 17),
        name="early_sum",
    )(*[arrived[step] for step in early])
    given = [total] + [arrived[step] for step in late]
    border = pl.pallas_call(
        functools.partial(border_kernel, capacity, LATE),
        out_shape=jax.ShapeDtypeStruct((TR, 2 * side, side), bf16),
        in_specs=[ANY] * len(given),
        out_specs=VMEM,
        scratch_shapes=[pltpu.VMEM((TR + 1, 2 * side, side), f32)]
        + held(LATE)
        + [pltpu.SemaphoreType.DMA((TR + LATE,))],
        name="border_sum",
    )(*given)
    border = passed_along(border, owners)
    sky = jax.ShapeDtypeStruct((TR * side, TC * side), f32)
    coadd, weight_map, edge = pl.pallas_call(
        functools.partial(inner_kernel, capacity, LATE),
        out_shape=[sky, sky, jax.ShapeDtypeStruct((TR, 2 * side, side), f32)],
        in_specs=[ANY] * len(given),
        out_specs=[VMEM] * 3,
        scratch_shapes=[pltpu.VMEM(totals, f32)]
        + held(LATE)
        + [pltpu.SemaphoreType.DMA((1 + LATE,))],
        cost_estimate=cost(1, 1 << 22, 1 << 23),
        name="inner",
    )(*given)
    return tuple(
        pl.pallas_call(
            edge_kernel,
            out_shape=[sky, sky],
            in_specs=[VMEM] * 2 + [ANY] * 2,
            out_specs=[ANY] * 2,
            scratch_shapes=[pltpu.VMEM((TR, side, side), f32)] * 2
            + [pltpu.SemaphoreType.DMA((2, TR))],
            input_output_aliases={2: 0, 3: 1},
            name="edge",
        )(edge, border, coadd, weight_map)
    )


def solution(mesh):
    placed = (
        P(("grp", "ra"), None, None),
        P(("grp", "ra"), None, None),
        P(("grp", "ra"), None, None),
        P(),
        P(("grp", "ra"), None),
        P(("grp", "ra"), None),
        P(("grp", "ra")),
        P(("grp", "ra")),
    )
    return jax.shard_map(
        shards,
        mesh=mesh,
        in_specs=placed,
        out_specs=(P("grp", "ra"), P("grp", "ra")),
        check_vma=False,
    )
```

```python
import functools

import jax
import jax.numpy as jnp
from jax import lax
from jax.experimental import pallas as pl
from jax.experimental.pallas import tpu as pltpu
from jax.sharding import PartitionSpec as P

TR = 4
TC = 4
TILES = TR * (TC + 1)
IDS = 16
LATE = 2

SMEM = pl.BlockSpec(memory_space=pltpu.SMEM)
VMEM = pl.BlockSpec(memory_space=pltpu.VMEM)
ANY = pl.BlockSpec(memory_space=pl.ANY)

WHOLE = pltpu.CompilerParams(vmem_limit_bytes=67_000_000)


def dot(left, right):
    return jnp.dot(left, right, preferred_element_type=jnp.float32)


def dot_t(left, right):
    return lax.dot_general(
        left, right, (((1,), (1,)), ((), ())), preferred_element_type=jnp.float32
    )


def lanes():
    return lax.broadcasted_iota(jnp.int32, (8, 128), 1)


def staggered(row):
    return pltpu.roll(jnp.broadcast_to(row, (8, 128)), 0, 1, stride=1, stride_axis=0)


def tap_lines(taps, order, slots):
    ntaps, kinds, blocks = taps.shape
    flat = taps[...].reshape(ntaps * kinds, blocks)
    rows = -(-len(slots) // 16) * 16
    which = lax.broadcasted_iota(jnp.int32, (rows, blocks), 0)
    wanted = jnp.full((rows, blocks), -1, jnp.int32)
    for index, slot in enumerate(slots):
        wanted = jnp.where(which == index, order[slot], wanted)
    pick = wanted == lax.broadcasted_iota(jnp.int32, (rows, blocks), 1)
    mixed = dot_t(pick.astype(jnp.float32).astype(jnp.bfloat16), flat).astype(jnp.bfloat16)
    shape = (ntaps * kinds, kinds * 128)
    source = lax.broadcasted_iota(jnp.int32, shape, 0)
    lane = lax.broadcasted_iota(jnp.int32, shape, 1)
    moved = source == (lane % 128) * kinds + lane // 128
    moved &= lane % 128 < ntaps
    return dot(mixed, moved.astype(jnp.float32).astype(jnp.bfloat16))


def banded(taps, side, wide):
    base, ntaps = staggered(taps), wide - side + 1
    low, high = [], []
    for start in range(0, side, 8):
        turned = pltpu.roll(base, start, 1) if start else base
        if start + 7 + ntaps <= 128:
            low.append(turned)
            high.append(jnp.zeros_like(turned))
        else:
            low.append(jnp.where(lanes() >= 64, turned, 0.0))
            high.append(jnp.where(lanes() >= 64, 0.0, turned))
    both = jnp.concatenate([jnp.concatenate(low, 0), jnp.concatenate(high, 0)], 1)
    return both.astype(jnp.bfloat16)[:, :wide]


def slots_body(owners, capacity, count, dest, row, col, order, ids):
    me = lax.axis_index("ra")

    def clear(slot, carry):
        order[slot] = 0
        ids[slot] = TILES
        return carry

    lax.fori_loop(0, owners * capacity, clear, 0)

    def zero(owner, carry):
        count[owner] = 0
        return carry

    lax.fori_loop(0, owners, zero, 0)

    def place(block, carry):
        owner = dest[block]
        rank = count[owner]
        count[owner] = rank + 1
        slot = (owner ^ me) * capacity + rank
        order[slot] = block
        ids[slot] = row[block] * (TC + 1) + col[block]
        return carry

    lax.fori_loop(0, dest.shape[0], place, 0)


def blocks_body(capacity, steps, order, ids, widx, arrays, outs, buffers, sem, meanwhile=None):
    taps, pixels, ivar, table = arrays
    px, iv, rt, ct = buffers
    side, wide = ivar.shape[1], pixels.shape[1]
    copies = []
    for index, step in enumerate(steps):
        for rank in range(capacity):
            at = index * capacity + rank
            block = order[step * capacity + rank]
            pairs = (
                (pixels.at[block], px.at[at]),
                (ivar.at[block], iv.at[at]),
                (table.at[widx[0, block]], rt.at[at]),
                (table.at[widx[1, block]], ct.at[at]),
            )
            for kind, (source, target) in enumerate(pairs):
                copy = pltpu.make_async_copy(source, target, sem.at[kind, at])
                copy.start()
                copies.append(copy)
    if meanwhile is not None:
        meanwhile()
    slots = [step * capacity + rank for step in steps for rank in range(capacity)]
    lines = tap_lines(taps, order, slots)
    for index, (step, out) in enumerate(zip(steps, outs)):
        at = range(index * capacity, (index + 1) * capacity)
        for copy in copies[4 * at[0] : 4 * (at[-1] + 1)]:
            copy.wait()
        cols = [banded(lines[i : i + 1, 128:], side, wide) for i in at]
        rows = [banded(lines[i : i + 1, :128], side, wide) for i in at]
        passed = [dot_t(px[i], k).astype(jnp.bfloat16) for i, k in zip(at, cols)]
        weighted = [
            (dot(k, p) * iv[i].astype(jnp.float32)).astype(jnp.bfloat16)
            for i, k, p in zip(at, rows, passed)
        ]
        middle = [
            dot(rt[i], jnp.concatenate([w, iv[i]], 1)).astype(jnp.bfloat16)
            for i, w in zip(at, weighted)
        ]
        for rank, (i, m) in enumerate(zip(at, middle)):
            both = jnp.concatenate([m[:, :side], m[:, side:]], 0)
            out[pl.ds(rank * 2 * side, 2 * side), :] = dot_t(both, ct[i]).astype(jnp.bfloat16)
        which = lax.broadcasted_iota(jnp.int32, (IDS, side), 0)
        tiles = jnp.full((IDS, side), TILES, jnp.int32)
        for rank in range(capacity):
            tiles = jnp.where(which == rank, ids[step * capacity + rank], tiles)
        out[pl.ds(capacity * 2 * side, IDS), :] = tiles.astype(jnp.float32).astype(jnp.bfloat16)


def first_kernel(owners, capacity, steps, *refs):
    dest, row, col, widx = refs[:4]
    arrays, refs = refs[4:8], refs[8:]
    order, ids = refs[:2]
    outs, refs = refs[2 : 2 + len(steps)], refs[2 + len(steps) :]
    (step,) = steps
    first = lax.axis_index("ra") ^ step

    def find(block, rank):
        hit = dest[block] == first

        @pl.when(hit)
        def _():
            order[step * capacity + rank] = block

        return rank + hit.astype(jnp.int32)

    for rank in range(capacity):
        order[step * capacity + rank] = 0
    lax.fori_loop(0, dest.shape[0], find, 0)
    fill = functools.partial(slots_body, owners, capacity, refs[-1], dest, row, col, order, ids)
    blocks_body(capacity, steps, order, ids, widx, arrays, outs, refs[:4], refs[4], fill)


def next_kernel(capacity, steps, *refs):
    order, ids, widx = refs[:3]
    arrays, refs = refs[3:7], refs[8:]
    outs, refs = refs[: len(steps)], refs[len(steps) :]
    blocks_body(capacity, steps, order, ids, widx, arrays, outs, refs[:4], refs[4])


def fetched(sources, targets, sem):
    copies = []
    for index, (source, target) in enumerate(zip(sources, targets)):
        copy = pltpu.make_async_copy(source, target, sem.at[index])
        copy.start()
        copies.append(copy)
    return copies


def add_parcel(parcel, capacity, side, add):
    for rank in range(capacity):
        tile = parcel[pl.ds(capacity * 2 * side, IDS), :].astype(jnp.float32)[rank : rank + 1]
        add(jnp.max(tile).astype(jnp.int32), parcel.at[pl.ds(rank * 2 * side, 2 * side), :])


def early_kernel(capacity, count, *refs):
    parcels, (total, buffer, sem) = refs[:count], refs[count:]
    side = total.shape[2]
    copies = fetched(parcels, [buffer.at[i] for i in range(count)], sem)
    total[...] = jnp.zeros_like(total)

    def add(tile, block):
        total[tile] = total[tile] + block[...].astype(jnp.float32)

    for index, copy in enumerate(copies):
        copy.wait()
        add_parcel(buffer.at[index], capacity, side, add)


def border_kernel(capacity, count, total, *refs):
    parcels, (border, sums, buffer, sem) = refs[:count], refs[count:]
    side = border.shape[2]
    columns = [total.at[row * (TC + 1) + TC] for row in range(TR)]
    targets = [sums.at[row] for row in range(TR)] + [buffer.at[i] for i in range(count)]
    for copy in fetched(columns + list(parcels), targets, sem):
        copy.wait()

    def add(tile, block):
        row = lax.select(lax.rem(tile, TC + 1) == TC, lax.div(tile, TC + 1), TR)
        sums[row] = sums[row] + block[...].astype(jnp.float32)

    sums[TR] = jnp.zeros_like(sums[TR])
    for index in range(count):
        add_parcel(buffer.at[index], capacity, side, add)
    for row in range(TR):
        border[row] = sums[row].astype(jnp.bfloat16)


def spots(row, col, side):
    return pl.ds(row * side, side), pl.ds(col * side, side)


def inner_kernel(capacity, count, total, *refs):
    parcels, (coadd, weight_map, edge, sums, buffer, sem) = refs[:count], refs[count:]
    side = edge.shape[2]
    targets = [sums] + [buffer.at[i] for i in range(count)]
    for copy in fetched([total] + list(parcels), targets, sem):
        copy.wait()

    def add(tile, block):
        sums[tile] = sums[tile] + block[...].astype(jnp.float32)

    for index in range(count):
        add_parcel(buffer.at[index], capacity, side, add)
    for row in range(TR):
        edge[row] = sums[row * (TC + 1)]
        for col in range(TC):
            both = sums[row * (TC + 1) + col]
            num, den = both[:side], both[side:]
            weight_map[spots(row, col, side)] = den
            coadd[spots(row, col, side)] = num / jnp.maximum(den, 1.0)


def edge_kernel(edge, border, coadd_in, map_in, coadd, weight_map, num, den, sem):
    side = edge.shape[2]
    copies = []
    for row in range(TR):
        both = edge[row] + border[row].astype(jnp.float32)
        num[row] = both[:side] / jnp.maximum(both[side:], 1.0)
        den[row] = both[side:]
        for kind, (source, target) in enumerate(((num, coadd), (den, weight_map))):
            copy = pltpu.make_async_copy(
                source.at[row], target.at[spots(row, 0, side)], sem.at[kind, row]
            )
            copy.start()
            copies.append(copy)
    for copy in copies:
        copy.wait()


def exchanged(value, owners, step):
    if step == 0:
        return value
    return lax.ppermute(value, "ra", [(source, source ^ step) for source in range(owners)])


def passed_along(value, owners):
    return lax.ppermute(value, "ra", [(source, (source + 1) % owners) for source in range(owners)])


def planned(owners):
    half = owners // 2
    far = list(range(half, owners))
    near = list(range(half - 1, -1, -1))
    steps = far[: half // 2] + near[: half // 4] + far[half // 2 : half // 2 + 2]
    steps += near[half // 4 : half // 2] + far[half // 2 + 2 :] + near[half // 2 :]
    groups = [steps[:1], steps[1:2], steps[2:4]]
    for start in range(4, owners, 3):
        groups.append(steps[start : start + 3])
    return groups, far


def shards(pixels, inverse_var, psf_taps, warp_table, warp_index, dest_patch, tile_row, tile_col):
    blocks, wide = pixels.shape[:2]
    side = inverse_var.shape[1]
    owners = lax.axis_size("ra")
    capacity = max(2, blocks // owners)
    bf16, f32 = jnp.bfloat16, jnp.float32
    parcel = jax.ShapeDtypeStruct((capacity * 2 * side + IDS, side), bf16)
    slots = jax.ShapeDtypeStruct((owners * capacity,), jnp.int32)
    totals = (TILES + 1, 2 * side, side)

    def cost(count, flops, moved):
        return pl.CostEstimate(flops=count * flops, bytes_accessed=count * moved, transcendentals=0)

    widx = warp_index.T
    arrays = (jnp.transpose(psf_taps, (2, 1, 0)), pixels, inverse_var, warp_table)
    groups, far = planned(owners)

    def buffers(count):
        return [
            pltpu.VMEM((count, wide, wide), bf16),
            pltpu.VMEM((count, side, side), bf16),
            pltpu.VMEM((count, side, side), bf16),
            pltpu.VMEM((count, side, side), bf16),
            pltpu.SemaphoreType.DMA((4, count)),
        ]

    sent = {}
    before = None
    for index, steps in enumerate(groups):
        count = len(steps) * capacity
        shared = dict(
            scratch_shapes=buffers(count),
            cost_estimate=cost(count, 30 << 20, 1 << 18),
            compiler_params=WHOLE,
            name="blocks_" + str(index),
        )
        if index == 0:
            shared["scratch_shapes"].append(pltpu.SMEM((owners,), jnp.int32))
            order, ids, *outs = pl.pallas_call(
                functools.partial(first_kernel, owners, capacity, steps),
                out_shape=[slots, slots] + [parcel] * len(steps),
                in_specs=[SMEM] * 4 + [VMEM] + [ANY] * 3,
                out_specs=[SMEM] * 2 + [VMEM] * len(steps),
                **shared,
            )(dest_patch[:, 0], tile_row, tile_col, widx, *arrays)
        else:
            outs = pl.pallas_call(
                functools.partial(next_kernel, capacity, steps),
                out_shape=[parcel] * len(steps),
                in_specs=[SMEM] * 3 + [VMEM] + [ANY] * 4,
                out_specs=[VMEM] * len(steps),
                **shared,
            )(order, ids, widx, *arrays, before)
        before = outs[0]
        sent.update(zip(steps, outs))
    steps = [step for group in groups for step in group]
    arrived = {step: exchanged(sent[step], owners, step) for step in steps}
    late = far[-LATE:]
    early = [step for step in steps if step not in late]

    def held(count):
        return [pltpu.VMEM((count,) + parcel.shape, bf16)]

    total = pl.pallas_call(
        functools.partial(early_kernel, capacity, len(early)),
        out_shape=jax.ShapeDtypeStruct(totals, f32),
        in_specs=[ANY] * len(early),
        out_specs=VMEM,
        scratch_shapes=held(len(early)) + [pltpu.SemaphoreType.DMA((len(early),))],
        cost_estimate=cost(len(early) * capacity, 1 << 16, 1 << 17),
        compiler_params=WHOLE,
        name="early_sum",
    )(*[arrived[step] for step in early])
    given = [total] + [arrived[step] for step in late]
    border = pl.pallas_call(
        functools.partial(border_kernel, capacity, LATE),
        out_shape=jax.ShapeDtypeStruct((TR, 2 * side, side), bf16),
        in_specs=[ANY] * len(given),
        out_specs=VMEM,
        scratch_shapes=[pltpu.VMEM((TR + 1, 2 * side, side), f32)]
        + held(LATE)
        + [pltpu.SemaphoreType.DMA((TR + LATE,))],
        compiler_params=WHOLE,
        name="border_sum",
    )(*given)
    border = passed_along(border, owners)
    sky = jax.ShapeDtypeStruct((TR * side, TC * side), f32)
    coadd, weight_map, edge = pl.pallas_call(
        functools.partial(inner_kernel, capacity, LATE),
        out_shape=[sky, sky, jax.ShapeDtypeStruct((TR, 2 * side, side), f32)],
        in_specs=[ANY] * len(given),
        out_specs=[VMEM] * 3,
        scratch_shapes=[pltpu.VMEM(totals, f32)]
        + held(LATE)
        + [pltpu.SemaphoreType.DMA((1 + LATE,))],
        cost_estimate=cost(1, 1 << 22, 1 << 23),
        compiler_params=WHOLE,
        name="inner",
    )(*given)
    return tuple(
        pl.pallas_call(
            edge_kernel,
            out_shape=[sky, sky],
            in_specs=[VMEM] * 2 + [ANY] * 2,
            out_specs=[ANY] * 2,
            scratch_shapes=[pltpu.VMEM((TR, side, side), f32)] * 2
            + [pltpu.SemaphoreType.DMA((2, TR))],
            input_output_aliases={2: 0, 3: 1},
            compiler_params=WHOLE,
            name="edge",
        )(edge, border, coadd, weight_map)
    )


def solution(mesh):
    placed = (
        P(("grp", "ra"), None, None),
        P(("grp", "ra"), None, None),
        P(("grp", "ra"), None, None),
        P(),
        P(("grp", "ra"), None),
        P(("grp", "ra"), None),
        P(("grp", "ra")),
        P(("grp", "ra")),
    )
    return jax.shard_map(
        shards,
        mesh=mesh,
        in_specs=placed,
        out_specs=(P("grp", "ra"), P("grp", "ra")),
        check_vma=False,
    )
```

```python
import functools

import jax
import jax.numpy as jnp
from jax import lax
from jax.experimental import pallas as pl
from jax.experimental.pallas import tpu as pltpu
from jax.sharding import PartitionSpec as P


TR = 4
TC = 4
TILES = TR * (TC + 1)
IDS = 16
LATE = 2

SMEM = pl.BlockSpec(memory_space=pltpu.SMEM)
VMEM = pl.BlockSpec(memory_space=pltpu.VMEM)
ANY = pl.BlockSpec(memory_space=pl.ANY)

WHOLE = pltpu.CompilerParams(vmem_limit_bytes=67_000_000)


def dot(left, right):
    return jnp.dot(left, right, preferred_element_type=jnp.float32)


def dot_t(left, right):
    return lax.dot_general(
        left, right, (((1,), (1,)), ((), ())), preferred_element_type=jnp.float32
    )


def lanes():
    return lax.broadcasted_iota(jnp.int32, (8, 128), 1)


def staggered(row):
    return pltpu.roll(jnp.broadcast_to(row, (8, 128)), 0, 1, stride=1, stride_axis=0)


def tap_lines(taps, order, slots):
    ntaps, kinds, blocks = taps.shape
    flat = taps[...].reshape(ntaps * kinds, blocks)
    rows = -(-len(slots) // 16) * 16
    which = lax.broadcasted_iota(jnp.int32, (rows, blocks), 0)
    wanted = jnp.full((rows, blocks), -1, jnp.int32)
    for index, slot in enumerate(slots):
        wanted = jnp.where(which == index, order[slot], wanted)
    pick = wanted == lax.broadcasted_iota(jnp.int32, (rows, blocks), 1)
    mixed = dot_t(pick.astype(jnp.float32).astype(jnp.bfloat16), flat).astype(jnp.bfloat16)
    shape = (ntaps * kinds, kinds * 128)
    source = lax.broadcasted_iota(jnp.int32, shape, 0)
    lane = lax.broadcasted_iota(jnp.int32, shape, 1)
    moved = source == (lane % 128) * kinds + lane // 128
    moved &= lane % 128 < ntaps
    return dot(mixed, moved.astype(jnp.float32).astype(jnp.bfloat16))


def banded(taps, side, wide):
    base, ntaps = staggered(taps), wide - side + 1
    low, high = [], []
    for start in range(0, side, 8):
        turned = pltpu.roll(base, start, 1) if start else base
        if start + 7 + ntaps <= 128:
            low.append(turned)
            high.append(jnp.zeros_like(turned))
        else:
            low.append(jnp.where(lanes() >= 64, turned, 0.0))
            high.append(jnp.where(lanes() >= 64, 0.0, turned))
    both = jnp.concatenate([jnp.concatenate(low, 0), jnp.concatenate(high, 0)], 1)
    return both.astype(jnp.bfloat16)[:, :wide]


def slots_body(owners, capacity, count, dest, row, col, order, ids):
    me = lax.axis_index("ra")

    def clear(slot, carry):
        order[slot] = 0
        ids[slot] = TILES
        return carry

    lax.fori_loop(0, owners * capacity, clear, 0)

    def zero(owner, carry):
        count[owner] = 0
        return carry

    lax.fori_loop(0, owners, zero, 0)

    def place(block, carry):
        owner = dest[block]
        rank = count[owner]
        count[owner] = rank + 1
        slot = (owner ^ me) * capacity + rank
        order[slot] = block
        ids[slot] = row[block] * (TC + 1) + col[block]
        return carry

    lax.fori_loop(0, dest.shape[0], place, 0)


def routed(tile, route):
    if route == "all":
        return tile
    border = lax.rem(tile, TC + 1) == TC
    if route == "inner":
        return lax.select(border, TILES, tile)
    return lax.select(border, tile - TC, TILES)


def blocks_body(capacity, pieces, order, ids, widx, arrays, outs, buffers, sem, meanwhile=None):
    taps, pixels, ivar, table = arrays
    px, iv, rt, ct = buffers
    side, wide = ivar.shape[1], pixels.shape[1]
    copies = []
    steps = sorted(set(step for step, _, _ in pieces), key=[p[0] for p in pieces].index)
    for index, step in enumerate(steps):
        for rank in range(capacity):
            at = index * capacity + rank
            block = order[step * capacity + rank]
            pairs = (
                (pixels.at[block], px.at[at]),
                (ivar.at[block], iv.at[at]),
                (table.at[widx[0, block]], rt.at[at]),
                (table.at[widx[1, block]], ct.at[at]),
            )
            for kind, (source, target) in enumerate(pairs):
                copy = pltpu.make_async_copy(source, target, sem.at[kind, at])
                copy.start()
                copies.append(copy)
    if meanwhile is not None:
        meanwhile()
    slots = [step * capacity + rank for step in steps for rank in range(capacity)]
    lines = tap_lines(taps, order, slots)
    for index, step in enumerate(steps):
        at = range(index * capacity, (index + 1) * capacity)
        for copy in copies[4 * at[0] : 4 * (at[-1] + 1)]:
            copy.wait()
        cols = [banded(lines[i : i + 1, 128:], side, wide) for i in at]
        rows = [banded(lines[i : i + 1, :128], side, wide) for i in at]
        passed = [dot_t(px[i], k).astype(jnp.bfloat16) for i, k in zip(at, cols)]
        weighted = [
            (dot(k, p) * iv[i].astype(jnp.float32)).astype(jnp.bfloat16)
            for i, k, p in zip(at, rows, passed)
        ]
        middle = [
            dot(rt[i], jnp.concatenate([w, iv[i]], 1)).astype(jnp.bfloat16)
            for i, w in zip(at, weighted)
        ]
        result = []
        for i, m in zip(at, middle):
            both = jnp.concatenate([m[:, :side], m[:, side:]], 0)
            result.append(dot_t(both, ct[i]).astype(jnp.bfloat16))
        which = lax.broadcasted_iota(jnp.int32, (IDS, side), 0)
        for (owner, ranks, route), out in zip(pieces, outs):
            if owner != step:
                continue
            tiles = jnp.full((IDS, side), TILES, jnp.int32)
            for place, rank in enumerate(ranks):
                out[pl.ds(place * 2 * side, 2 * side), :] = result[rank]
                tile = routed(ids[step * capacity + rank], route)
                tiles = jnp.where(which == place, tile, tiles)
            at_end = pl.ds(len(ranks) * 2 * side, IDS)
            out[at_end, :] = tiles.astype(jnp.float32).astype(jnp.bfloat16)


def first_kernel(owners, capacity, pieces, *refs):
    dest, row, col, widx = refs[:4]
    arrays, refs = refs[4:8], refs[8:]
    order, ids = refs[:2]
    outs, refs = refs[2 : 2 + len(pieces)], refs[2 + len(pieces) :]
    step = pieces[0][0]
    first = lax.axis_index("ra") ^ step

    def find(block, rank):
        hit = dest[block] == first

        @pl.when(hit)
        def _():
            order[step * capacity + rank] = block

        return rank + hit.astype(jnp.int32)

    for rank in range(capacity):
        order[step * capacity + rank] = 0
    lax.fori_loop(0, dest.shape[0], find, 0)
    fill = functools.partial(slots_body, owners, capacity, refs[-1], dest, row, col, order, ids)
    blocks_body(capacity, pieces, order, ids, widx, arrays, outs, refs[:4], refs[4], fill)


def next_kernel(capacity, pieces, *refs):
    order, ids, widx = refs[:3]
    arrays, refs = refs[3:7], refs[8:]
    outs, refs = refs[: len(pieces)], refs[len(pieces) :]
    blocks_body(capacity, pieces, order, ids, widx, arrays, outs, refs[:4], refs[4])


def fetched(sources, targets, sem):
    copies = []
    for index, (source, target) in enumerate(zip(sources, targets)):
        copy = pltpu.make_async_copy(source, target, sem.at[index])
        copy.start()
        copies.append(copy)
    return copies


def add_parcel(parcel, side, add):
    count = parcel.shape[0] // (2 * side)
    tiles = parcel[pl.ds(count * 2 * side, IDS), :].astype(jnp.float32)
    for rank in range(count):
        tile = tiles[rank : rank + 1]
        add(jnp.max(tile).astype(jnp.int32), parcel.at[pl.ds(rank * 2 * side, 2 * side), :])


def early_kernel(count, *refs):
    parcels, (total, *buffer, sem) = refs[:count], refs[count:]
    side = total.shape[2]
    copies = fetched(parcels, buffer, sem)
    total[...] = jnp.zeros_like(total)

    def add(tile, block):
        total[tile] = total[tile] + block[...].astype(jnp.float32)

    for index, copy in enumerate(copies):
        copy.wait()
        add_parcel(buffer[index], side, add)


def border_kernel(count, total, *refs):
    parcels, (border, sums, *buffer, sem) = refs[:count], refs[count:]
    side = border.shape[2]
    columns = [total.at[row * (TC + 1) + TC] for row in range(TR)]
    targets = [sums.at[row] for row in range(TR)] + buffer
    for copy in fetched(columns + list(parcels), targets, sem):
        copy.wait()

    def add(tile, block):
        row = lax.select(lax.rem(tile, TC + 1) == TC, lax.div(tile, TC + 1), TR)
        sums[row] = sums[row] + block[...].astype(jnp.float32)

    sums[TR] = jnp.zeros_like(sums[TR])
    for index in range(count):
        add_parcel(buffer[index], side, add)
    for row in range(TR):
        border[row] = sums[row].astype(jnp.bfloat16)


def spots(row, col, side):
    return pl.ds(row * side, side), pl.ds(col * side, side)


def inner_kernel(count, total, *refs):
    parcels, (coadd, weight_map, edge, sums, *buffer, sem) = refs[:count], refs[count:]
    side = edge.shape[2]
    for copy in fetched([total] + list(parcels), [sums] + buffer, sem):
        copy.wait()

    def add(tile, block):
        sums[tile] = sums[tile] + block[...].astype(jnp.float32)

    for index in range(count):
        add_parcel(buffer[index], side, add)
    for row in range(TR):
        edge[row] = sums[row * (TC + 1)]
        for col in range(TC):
            both = sums[row * (TC + 1) + col]
            num, den = both[:side], both[side:]
            weight_map[spots(row, col, side)] = den
            coadd[spots(row, col, side)] = num / jnp.maximum(den, 1.0)


def edge_kernel(edge, border, coadd_in, map_in, coadd, weight_map, num, den, sem):
    side = edge.shape[2]
    copies = []
    for row in range(TR):
        both = edge[row] + border[row].astype(jnp.float32)
        num[row] = both[:side] / jnp.maximum(both[side:], 1.0)
        den[row] = both[side:]
        for kind, (source, target) in enumerate(((num, coadd), (den, weight_map))):
            copy = pltpu.make_async_copy(
                source.at[row], target.at[spots(row, 0, side)], sem.at[kind, row]
            )
            copy.start()
            copies.append(copy)
    for copy in copies:
        copy.wait()


def exchanged(value, owners, step, beyond=0):
    if step == 0 and not beyond:
        return value
    pairs = [(source, ((source ^ step) + beyond) % owners) for source in range(owners)]
    return lax.ppermute(value, "ra", pairs)


def passed_along(value, owners):
    return lax.ppermute(value, "ra", [(source, (source + 1) % owners) for source in range(owners)])


def planned(owners):
    half = owners // 2
    far = list(range(half, owners))
    near = list(range(half - 1, -1, -1))
    over = near[: half // 2]
    cut = len(over) * 3 // 4
    steps = far[:3] + over[:cut] + far[3:4] + over[cut:] + far[4:] + near[half // 2 :]
    groups = [steps[:1], steps[1:2], steps[2:4]]
    for start in range(4, owners, 3):
        groups.append(steps[start : start + 3])
    return groups, far


def shards(pixels, inverse_var, psf_taps, warp_table, warp_index, dest_patch, tile_row, tile_col):
    blocks, wide = pixels.shape[:2]
    side = inverse_var.shape[1]
    owners = lax.axis_size("ra")
    capacity = max(2, blocks // owners)
    bf16, f32 = jnp.bfloat16, jnp.float32
    slots = jax.ShapeDtypeStruct((owners * capacity,), jnp.int32)
    totals = (TILES + 1, 2 * side, side)

    def cost(count, flops, moved):
        return pl.CostEstimate(flops=count * flops, bytes_accessed=count * moved, transcendentals=0)

    widx = warp_index.T
    arrays = (jnp.transpose(psf_taps, (2, 1, 0)), pixels, inverse_var, warp_table)
    groups, far = planned(owners)

    def buffers(count):
        return [
            pltpu.VMEM((count, wide, wide), bf16),
            pltpu.VMEM((count, side, side), bf16),
            pltpu.VMEM((count, side, side), bf16),
            pltpu.VMEM((count, side, side), bf16),
            pltpu.SemaphoreType.DMA((4, count)),
        ]

    def parcel(count):
        return jax.ShapeDtypeStruct((count * 2 * side + IDS, side), bf16)

    last = far[-1]
    everything, final = tuple(range(capacity)), (capacity - 1,)
    cut = [(last, everything[:-1], "all"), (last, final, "inner"), (last, final, "border")]
    sent = {}
    before = None
    for index, steps in enumerate(groups):
        count = len(steps) * capacity
        pieces = []
        for step in steps:
            pieces += cut if step == last else [(step, everything, "all")]
        parcels = [parcel(len(ranks)) for _, ranks, _ in pieces]
        shared = dict(
            scratch_shapes=buffers(count),
            cost_estimate=cost(count, 30 << 20, 1 << 18),
            compiler_params=WHOLE,
            name="blocks_" + str(index),
        )
        if index == 0:
            shared["scratch_shapes"].append(pltpu.SMEM((owners,), jnp.int32))
            order, ids, *outs = pl.pallas_call(
                functools.partial(first_kernel, owners, capacity, pieces),
                out_shape=[slots, slots] + parcels,
                in_specs=[SMEM] * 4 + [VMEM] + [ANY] * 3,
                out_specs=[SMEM] * 2 + [VMEM] * len(parcels),
                **shared,
            )(dest_patch[:, 0], tile_row, tile_col, widx, *arrays)
        else:
            outs = pl.pallas_call(
                functools.partial(next_kernel, capacity, pieces),
                out_shape=parcels,
                in_specs=[SMEM] * 3 + [VMEM] + [ANY] * 4,
                out_specs=[VMEM] * len(parcels),
                **shared,
            )(order, ids, widx, *arrays, before)
        before = outs[0]
        sent.update({(step, route): out for (step, _, route), out in zip(pieces, outs)})
    steps = [step for group in groups for step in group]
    arrived = {step: exchanged(sent[step, "all"], owners, step) for step in steps}
    late = [arrived[step] for step in far[-LATE:]]
    early = [arrived[step] for step in steps if step not in far[-LATE:]]
    ending = []
    for route, beyond in (("inner", 0), ("border", 1)):
        ending.append(exchanged(sent[last, route], owners, last, beyond))

    def held(parcels, others):
        scratch = [pltpu.VMEM(value.shape, bf16) for value in parcels]
        return scratch + [pltpu.SemaphoreType.DMA((len(parcels) + others,))]

    total = pl.pallas_call(
        functools.partial(early_kernel, len(early)),
        out_shape=jax.ShapeDtypeStruct(totals, f32),
        in_specs=[ANY] * len(early),
        out_specs=VMEM,
        scratch_shapes=held(early, 0),
        cost_estimate=cost(len(early) * capacity, 1 << 16, 1 << 17),
        compiler_params=WHOLE,
        name="early_sum",
    )(*early)
    border = pl.pallas_call(
        functools.partial(border_kernel, len(late)),
        out_shape=jax.ShapeDtypeStruct((TR, 2 * side, side), bf16),
        in_specs=[ANY] * (1 + len(late)),
        out_specs=VMEM,
        scratch_shapes=[pltpu.VMEM((TR + 1, 2 * side, side), f32)] + held(late, TR),
        compiler_params=WHOLE,
        name="border_sum",
    )(total, *late)
    border = passed_along(border, owners)
    rest = late + ending
    sky = jax.ShapeDtypeStruct((TR * side, TC * side), f32)
    coadd, weight_map, edge = pl.pallas_call(
        functools.partial(inner_kernel, len(rest)),
        out_shape=[sky, sky, jax.ShapeDtypeStruct((TR, 2 * side, side), f32)],
        in_specs=[ANY] * (1 + len(rest)),
        out_specs=[VMEM] * 3,
        scratch_shapes=[pltpu.VMEM(totals, f32)] + held(rest, 1),
        cost_estimate=cost(1, 1 << 22, 1 << 23),
        compiler_params=WHOLE,
        name="inner",
    )(total, *rest)
    return tuple(
        pl.pallas_call(
            edge_kernel,
            out_shape=[sky, sky],
            in_specs=[VMEM] * 2 + [ANY] * 2,
            out_specs=[ANY] * 2,
            scratch_shapes=[pltpu.VMEM((TR, side, side), f32)] * 2
            + [pltpu.SemaphoreType.DMA((2, TR))],
            input_output_aliases={2: 0, 3: 1},
            compiler_params=WHOLE,
            name="edge",
        )(edge, border, coadd, weight_map)
    )


def solution(mesh):
    placed = (
        P(("grp", "ra"), None, None),
        P(("grp", "ra"), None, None),
        P(("grp", "ra"), None, None),
        P(),
        P(("grp", "ra"), None),
        P(("grp", "ra"), None),
        P(("grp", "ra")),
        P(("grp", "ra")),
    )
    return jax.shard_map(
        shards,
        mesh=mesh,
        in_specs=placed,
        out_specs=(P("grp", "ra"), P("grp", "ra")),
        check_vma=False,
    )
```

```python
import functools

import jax
import jax.numpy as jnp
from jax import lax
from jax.experimental import pallas as pl
from jax.experimental.pallas import tpu as pltpu
from jax.sharding import PartitionSpec as P


TR = 4
TC = 4
TILES = TR * (TC + 1)
IDS = 8
LATE = 2
LATE_OVER = 0
BYPASS = 1

SMEM = pl.BlockSpec(memory_space=pltpu.SMEM)
VMEM = pl.BlockSpec(memory_space=pltpu.VMEM)
ANY = pl.BlockSpec(memory_space=pl.ANY)

WHOLE = pltpu.CompilerParams(vmem_limit_bytes=67_000_000)


def dot(left, right):
    return jnp.dot(left, right, preferred_element_type=jnp.float32)


def dot_t(left, right):
    return lax.dot_general(
        left, right, (((1,), (1,)), ((), ())), preferred_element_type=jnp.float32
    )


def lanes():
    return lax.broadcasted_iota(jnp.int32, (8, 128), 1)


def staggered(row):
    return pltpu.roll(jnp.broadcast_to(row, (8, 128)), 0, 1, stride=1, stride_axis=0)


def tap_lines(taps, order, slots):
    ntaps, kinds, blocks = taps.shape
    flat = taps[...].reshape(ntaps * kinds, blocks)
    rows = -(-len(slots) // 16) * 16
    which = lax.broadcasted_iota(jnp.int32, (rows, blocks), 0)
    wanted = jnp.full((rows, blocks), -1, jnp.int32)
    for index, slot in enumerate(slots):
        wanted = jnp.where(which == index, order[slot], wanted)
    pick = wanted == lax.broadcasted_iota(jnp.int32, (rows, blocks), 1)
    mixed = dot_t(pick.astype(jnp.float32).astype(jnp.bfloat16), flat).astype(jnp.bfloat16)
    shape = (ntaps * kinds, kinds * 128)
    source = lax.broadcasted_iota(jnp.int32, shape, 0)
    lane = lax.broadcasted_iota(jnp.int32, shape, 1)
    moved = source == (lane % 128) * kinds + lane // 128
    moved &= lane % 128 < ntaps
    return dot(mixed, moved.astype(jnp.float32).astype(jnp.bfloat16))


def banded(taps, side, wide):
    base, ntaps = staggered(taps), wide - side + 1
    low, high = [], []
    for start in range(0, side, 8):
        turned = pltpu.roll(base, start, 1) if start else base
        if start + 7 + ntaps <= 128:
            low.append(turned)
            high.append(jnp.zeros_like(turned))
        else:
            low.append(jnp.where(lanes() >= 64, turned, 0.0))
            high.append(jnp.where(lanes() >= 64, 0.0, turned))
    both = jnp.concatenate([jnp.concatenate(low, 0), jnp.concatenate(high, 0)], 1)
    return both.astype(jnp.bfloat16)[:, :wide]


def slots_body(owners, capacity, count, dest, row, col, order, ids):
    me = lax.axis_index("ra")

    def clear(slot, carry):
        order[slot] = 0
        ids[slot] = TILES
        return carry

    lax.fori_loop(0, owners * capacity, clear, 0)

    def zero(owner, carry):
        count[owner] = 0
        return carry

    lax.fori_loop(0, owners, zero, 0)

    def place(block, carry):
        owner = dest[block]
        rank = count[owner]
        count[owner] = rank + 1
        slot = (owner ^ me) * capacity + rank
        order[slot] = block
        ids[slot] = row[block] * (TC + 1) + col[block]
        return carry

    lax.fori_loop(0, dest.shape[0], place, 0)


def routed(tile, route):
    if route == "all":
        return tile
    border = lax.rem(tile, TC + 1) == TC
    if route == "inner":
        return lax.select(border, TILES, tile)
    return lax.select(border, tile - TC, TILES)


def blocks_body(capacity, pieces, order, ids, widx, arrays, outs, buffers, sem, meanwhile=None):
    taps, pixels, ivar, table = arrays
    px, iv, rt, ct = buffers
    side, wide = ivar.shape[1], pixels.shape[1]
    copies = []
    steps = sorted(set(step for step, _, _ in pieces), key=[p[0] for p in pieces].index)
    for index, step in enumerate(steps):
        for rank in range(capacity):
            at = index * capacity + rank
            block = order[step * capacity + rank]
            pairs = (
                (pixels.at[block], px.at[at]),
                (ivar.at[block], iv.at[at]),
                (table.at[widx[0, block]], rt.at[at]),
                (table.at[widx[1, block]], ct.at[at]),
            )
            for kind, (source, target) in enumerate(pairs):
                copy = pltpu.make_async_copy(source, target, sem.at[kind, at])
                copy.start()
                copies.append(copy)
    if meanwhile is not None:
        meanwhile()
    slots = [step * capacity + rank for step in steps for rank in range(capacity)]
    lines = tap_lines(taps, order, slots)
    for index, step in enumerate(steps):
        at = range(index * capacity, (index + 1) * capacity)
        for copy in copies[4 * at[0] : 4 * (at[-1] + 1)]:
            copy.wait()
        cols = [banded(lines[i : i + 1, 128:], side, wide) for i in at]
        rows = [banded(lines[i : i + 1, :128], side, wide) for i in at]
        passed = [dot_t(px[i], k).astype(jnp.bfloat16) for i, k in zip(at, cols)]
        weighted = [
            (dot(k, p) * iv[i].astype(jnp.float32)).astype(jnp.bfloat16)
            for i, k, p in zip(at, rows, passed)
        ]
        middle = [
            dot(rt[i], jnp.concatenate([w, iv[i]], 1)).astype(jnp.bfloat16)
            for i, w in zip(at, weighted)
        ]
        result = []
        for i, m in zip(at, middle):
            both = jnp.concatenate([m[:, :side], m[:, side:]], 0)
            result.append(dot_t(both, ct[i]).astype(jnp.bfloat16))
        which = lax.broadcasted_iota(jnp.int32, (IDS, side), 0)
        for (owner, ranks, route), out in zip(pieces, outs):
            if owner != step:
                continue
            tiles = jnp.full((IDS, side), TILES, jnp.int32)
            for place, rank in enumerate(ranks):
                out[pl.ds(place * 2 * side, 2 * side), :] = result[rank]
                tile = routed(ids[step * capacity + rank], route)
                tiles = jnp.where(which == place, tile, tiles)
            at_end = pl.ds(len(ranks) * 2 * side, IDS)
            out[at_end, :] = tiles.astype(jnp.float32).astype(jnp.bfloat16)


def first_kernel(owners, capacity, pieces, *refs):
    dest, row, col, widx = refs[:4]
    arrays, refs = refs[4:8], refs[8:]
    order, ids = refs[:2]
    outs, refs = refs[2 : 2 + len(pieces)], refs[2 + len(pieces) :]
    step = pieces[0][0]
    first = lax.axis_index("ra") ^ step

    base = step * capacity
    for rank in range(capacity):
        refs[-2][rank] = 0
    rank = jnp.int32(0)
    for block in range(dest.shape[0]):
        refs[-2][rank] = block
        rank = rank + (dest[block] == first).astype(jnp.int32)
    for place in range(capacity):
        order[base + place] = lax.select(place < rank, refs[-2][place], 0)
    fill = functools.partial(slots_body, owners, capacity, refs[-1], dest, row, col, order, ids)
    blocks_body(capacity, pieces, order, ids, widx, arrays, outs, refs[:4], refs[4], fill)


def next_kernel(capacity, pieces, *refs):
    order, ids, widx = refs[:3]
    arrays, refs = refs[3:7], refs[8:]
    outs, refs = refs[: len(pieces)], refs[len(pieces) :]
    blocks_body(capacity, pieces, order, ids, widx, arrays, outs, refs[:4], refs[4])


def fetched(sources, targets, sem):
    copies = []
    for index, (source, target) in enumerate(zip(sources, targets)):
        copy = pltpu.make_async_copy(source, target, sem.at[index])
        copy.start()
        copies.append(copy)
    return copies


def add_parcel(parcel, side, add):
    count = parcel.shape[0] // (2 * side)
    tiles = parcel[pl.ds(count * 2 * side, IDS), :].astype(jnp.float32)
    for rank in range(count):
        tile = tiles[rank : rank + 1]
        add(jnp.max(tile).astype(jnp.int32), parcel.at[pl.ds(rank * 2 * side, 2 * side), :])


def early_kernel(count, *refs):
    parcels, (total, *buffer, sem) = refs[:count], refs[count:]
    side = total.shape[2]
    copies = fetched(parcels, buffer, sem)
    total[...] = jnp.zeros_like(total)

    def add(tile, block):
        total[tile] = total[tile] + block[...].astype(jnp.float32)

    for index, copy in enumerate(copies):
        copy.wait()
        add_parcel(buffer[index], side, add)


def border_kernel(count, total, *refs):
    parcels, (border, sums, *buffer, sem) = refs[:count], refs[count:]
    side = border.shape[2]
    columns = [total.at[row * (TC + 1) + TC] for row in range(TR)]
    targets = [sums.at[row] for row in range(TR)] + buffer
    for copy in fetched(columns + list(parcels), targets, sem):
        copy.wait()

    def add(tile, block):
        row = lax.select(lax.rem(tile, TC + 1) == TC, lax.div(tile, TC + 1), TR)
        sums[row] = sums[row] + block[...].astype(jnp.float32)

    sums[TR] = jnp.zeros_like(sums[TR])
    for index in range(count):
        add_parcel(buffer[index], side, add)
    for row in range(TR):
        border[row] = sums[row].astype(jnp.bfloat16)


def inner_kernel(count, total, *refs):
    parcels, (coadd, weight_map, edge, sums, ratio, weight, *buffer, sem, out_sem) = (
        refs[:count],
        refs[count:],
    )
    side = edge.shape[2]
    for copy in fetched([total] + list(parcels), [sums] + buffer, sem):
        copy.wait()

    def add(tile, block):
        sums[tile] = sums[tile] + block[...].astype(jnp.float32)

    for index in range(count):
        add_parcel(buffer[index], side, add)
    copies = []
    for row in range(TR):
        pairs = [(sums.at[row * (TC + 1)], edge.at[row])]
        for col in range(TC):
            both = sums[row * (TC + 1) + col]
            num, den = both[:side], both[side:]
            at = pl.ds(col * side, side)
            weight[row, :, at] = den
            ratio[row, :, at] = num / jnp.maximum(den, 1.0)
        rows = pl.ds(row * side, side)
        pairs += [(ratio.at[row], coadd.at[rows]), (weight.at[row], weight_map.at[rows])]
        for kind, (source, target) in enumerate(pairs):
            copies.append(pltpu.make_async_copy(source, target, out_sem.at[kind, row]))
            copies[-1].start()
    for copy in copies:
        copy.wait()


def edge_kernel(edge, border, coadd_in, map_in, coadd, weight_map, sums, more, num, den, sem, in_sem):
    side = edge.shape[2]
    sources = [edge.at[row] for row in range(TR)] + [border.at[row] for row in range(TR)]
    targets = [sums.at[row] for row in range(TR)] + [more.at[row] for row in range(TR)]
    arriving = fetched(sources, targets, in_sem)
    copies = []
    for row in range(TR):
        arriving[row].wait()
        arriving[TR + row].wait()
        both = sums[row] + more[row].astype(jnp.float32)
        num[row] = both[:side] / jnp.maximum(both[side:], 1.0)
        den[row] = both[side:]
        for kind, (source, target) in enumerate(((num, coadd), (den, weight_map))):
            copy = pltpu.make_async_copy(
                source.at[row],
                target.at[pl.ds(row * side, side), pl.ds(0, side)],
                sem.at[kind, row],
            )
            copy.start()
            copies.append(copy)
    for copy in copies:
        copy.wait()


def exchanged(value, owners, step, beyond=0):
    if step == 0 and not beyond:
        return value
    pairs = [(source, ((source ^ step) + beyond) % owners) for source in range(owners)]
    return lax.ppermute(value, "ra", pairs)


def passed_along(value, owners):
    return lax.ppermute(value, "ra", [(source, (source + 1) % owners) for source in range(owners)])


def planned(owners):
    half = owners // 2
    far = list(range(half, owners))
    near = list(range(half - 1, -1, -1))
    over, side = near[: half // 2], near[half // 2 : -2]
    cut = len(over) * 3 // 4
    steps = far[:3] + over[:cut] + far[3:4] + over[cut:] + far[4:5] + side + far[5:] + near[-2:]
    groups = [steps[:1], steps[1:2], steps[2:4]]
    for start in range(4, owners, 3):
        groups.append(steps[start : start + 3])
    groups[-1:] = [groups[-1][:1], groups[-1][1:]] if len(groups[-1]) > 1 else groups[-1:]
    return groups, far[-1], over[len(over) - LATE_OVER :] + far[len(far) - LATE :]


def shards(pixels, inverse_var, psf_taps, warp_table, warp_index, dest_patch, tile_row, tile_col):
    blocks, wide = pixels.shape[:2]
    side = inverse_var.shape[1]
    owners = lax.axis_size("ra")
    capacity = max(2, blocks // owners)
    bf16, f32 = jnp.bfloat16, jnp.float32
    slots = jax.ShapeDtypeStruct((owners * capacity,), jnp.int32)
    totals = (TILES + 1, 2 * side, side)

    def cost(count, flops, moved):
        return pl.CostEstimate(flops=count * flops, bytes_accessed=count * moved, transcendentals=0)

    widx = warp_index.T
    arrays = (jnp.transpose(psf_taps, (2, 1, 0)), pixels, inverse_var, warp_table)
    groups, last, slow = planned(owners)

    def buffers(count):
        return [
            pltpu.VMEM((count, wide, wide), bf16),
            pltpu.VMEM((count, side, side), bf16),
            pltpu.VMEM((count, side, side), bf16),
            pltpu.VMEM((count, side, side), bf16),
            pltpu.SemaphoreType.DMA((4, count)),
        ]

    def parcel(count):
        return jax.ShapeDtypeStruct((count * 2 * side + IDS, side), bf16)

    everything, kept = tuple(range(capacity)), capacity - min(BYPASS, capacity - 1)
    final = everything[kept:]
    cut = [(last, everything[:kept], "all"), (last, final, "inner"), (last, final, "border")]
    sent = {}
    before = None
    for index, steps in enumerate(groups):
        count = len(steps) * capacity
        pieces = []
        for step in steps:
            pieces += cut if step == last else [(step, everything, "all")]
        parcels = [parcel(len(ranks)) for _, ranks, _ in pieces]
        shared = dict(
            scratch_shapes=buffers(count),
            cost_estimate=cost(count, 30 << 20, 1 << 18),
            compiler_params=WHOLE,
            name="blocks_" + str(index),
        )
        if index == 0:
            shared["scratch_shapes"] += [
                pltpu.SMEM((capacity + 1,), jnp.int32),
                pltpu.SMEM((owners,), jnp.int32),
            ]
            order, ids, *outs = pl.pallas_call(
                functools.partial(first_kernel, owners, capacity, pieces),
                out_shape=[slots, slots] + parcels,
                in_specs=[SMEM] * 4 + [VMEM] + [ANY] * 3,
                out_specs=[SMEM] * 2 + [VMEM] * len(parcels),
                **shared,
            )(dest_patch[:, 0], tile_row, tile_col, widx, *arrays)
        else:
            outs = pl.pallas_call(
                functools.partial(next_kernel, capacity, pieces),
                out_shape=parcels,
                in_specs=[SMEM] * 3 + [VMEM] + [ANY] * 4,
                out_specs=[VMEM] * len(parcels),
                **shared,
            )(order, ids, widx, *arrays, before)
        before = outs[0]
        sent.update({(step, route): out for (step, _, route), out in zip(pieces, outs)})
    steps = [step for group in groups for step in group]
    arrived = {}
    for step in steps:
        arrived[step] = exchanged(sent[step, "all"], owners, step)
    late = [arrived[step] for step in slow]
    early = [arrived[step] for step in steps if step not in slow]
    ending = []
    for route, beyond in (("inner", 0), ("border", 1)):
        ending.append(exchanged(sent[last, route], owners, last, beyond))

    def held(parcels, others):
        scratch = [pltpu.VMEM(value.shape, bf16) for value in parcels]
        return scratch + [pltpu.SemaphoreType.DMA((len(parcels) + others,))]

    total = pl.pallas_call(
        functools.partial(early_kernel, len(early)),
        out_shape=jax.ShapeDtypeStruct(totals, f32),
        in_specs=[ANY] * len(early),
        out_specs=VMEM,
        scratch_shapes=held(early, 0),
        cost_estimate=cost(len(early) * capacity, 1 << 16, 1 << 17),
        compiler_params=WHOLE,
        name="early_sum",
    )(*early)
    border = pl.pallas_call(
        functools.partial(border_kernel, len(late)),
        out_shape=jax.ShapeDtypeStruct((TR, 2 * side, side), bf16),
        in_specs=[ANY] * (1 + len(late)),
        out_specs=VMEM,
        scratch_shapes=[pltpu.VMEM((TR + 1, 2 * side, side), f32)] + held(late, TR),
        compiler_params=WHOLE,
        name="border_sum",
    )(total, *late)
    border = passed_along(border, owners)
    rest = late + ending
    sky = jax.ShapeDtypeStruct((TR * side, TC * side), f32)
    coadd, weight_map, edge = pl.pallas_call(
        functools.partial(inner_kernel, len(rest)),
        out_shape=[sky, sky, jax.ShapeDtypeStruct((TR, 2 * side, side), f32)],
        in_specs=[ANY] * (1 + len(rest)),
        out_specs=[ANY] * 3,
        scratch_shapes=[pltpu.VMEM(totals, f32)]
        + [pltpu.VMEM((TR, side, TC * side), f32)] * 2
        + held(rest, 1)
        + [pltpu.SemaphoreType.DMA((3, TR))],
        cost_estimate=cost(1, 1 << 22, 1 << 23),
        compiler_params=WHOLE,
        name="inner",
    )(total, *rest)
    return tuple(
        pl.pallas_call(
            edge_kernel,
            out_shape=[sky, sky],
            in_specs=[ANY] * 4,
            out_specs=[ANY] * 2,
            scratch_shapes=[
                pltpu.VMEM((TR, 2 * side, side), f32),
                pltpu.VMEM((TR, 2 * side, side), bf16),
                pltpu.VMEM((TR, side, side), f32),
                pltpu.VMEM((TR, side, side), f32),
                pltpu.SemaphoreType.DMA((2, TR)),
                pltpu.SemaphoreType.DMA((2 * TR,)),
            ],
            input_output_aliases={2: 0, 3: 1},
            compiler_params=WHOLE,
            name="edge",
        )(edge, border, coadd, weight_map)
    )


def solution(mesh):
    placed = (
        P(("grp", "ra"), None, None),
        P(("grp", "ra"), None, None),
        P(("grp", "ra"), None, None),
        P(),
        P(("grp", "ra"), None),
        P(("grp", "ra"), None),
        P(("grp", "ra")),
        P(("grp", "ra")),
    )
    return jax.shard_map(
        shards,
        mesh=mesh,
        in_specs=placed,
        out_specs=(P("grp", "ra"), P("grp", "ra")),
        check_vma=False,
    )
```

```python
import functools

import jax
import jax.numpy as jnp
from jax import lax
from jax.experimental import pallas as pl
from jax.experimental.pallas import tpu as pltpu
from jax.sharding import PartitionSpec as P


TR = 4
TC = 4
TILES = TR * (TC + 1)
IDS = 8
LATE = 2
LATE_OVER = 0
BYPASS = 1

SMEM = pl.BlockSpec(memory_space=pltpu.SMEM)
VMEM = pl.BlockSpec(memory_space=pltpu.VMEM)
ANY = pl.BlockSpec(memory_space=pl.ANY)

WHOLE = pltpu.CompilerParams(vmem_limit_bytes=67_000_000)


def dot(left, right):
    return jnp.dot(left, right, preferred_element_type=jnp.float32)


def dot_t(left, right):
    return lax.dot_general(
        left, right, (((1,), (1,)), ((), ())), preferred_element_type=jnp.float32
    )


def lanes():
    return lax.broadcasted_iota(jnp.int32, (8, 128), 1)


def staggered(row):
    return pltpu.roll(jnp.broadcast_to(row, (8, 128)), 0, 1, stride=1, stride_axis=0)


def tap_lines(taps, order, slots):
    ntaps, kinds, blocks = taps.shape
    flat = taps[...].reshape(ntaps * kinds, blocks)
    rows = -(-len(slots) // 16) * 16
    which = lax.broadcasted_iota(jnp.int32, (rows, blocks), 0)
    wanted = jnp.full((rows, blocks), -1, jnp.int32)
    for index, slot in enumerate(slots):
        wanted = jnp.where(which == index, order[slot], wanted)
    pick = wanted == lax.broadcasted_iota(jnp.int32, (rows, blocks), 1)
    mixed = dot_t(pick.astype(jnp.float32).astype(jnp.bfloat16), flat).astype(jnp.bfloat16)
    shape = (ntaps * kinds, kinds * 128)
    source = lax.broadcasted_iota(jnp.int32, shape, 0)
    lane = lax.broadcasted_iota(jnp.int32, shape, 1)
    moved = source == (lane % 128) * kinds + lane // 128
    moved &= lane % 128 < ntaps
    return dot(mixed, moved.astype(jnp.float32).astype(jnp.bfloat16))


def banded(taps, side, wide):
    base, ntaps = staggered(taps), wide - side + 1
    low, high = [], []
    for start in range(0, side, 8):
        turned = pltpu.roll(base, start, 1) if start else base
        if start + 7 + ntaps <= 128:
            low.append(turned)
            high.append(jnp.zeros_like(turned))
        else:
            low.append(jnp.where(lanes() >= 64, turned, 0.0))
            high.append(jnp.where(lanes() >= 64, 0.0, turned))
    both = jnp.concatenate([jnp.concatenate(low, 0), jnp.concatenate(high, 0)], 1)
    return both.astype(jnp.bfloat16)[:, :wide]


def slots_body(owners, capacity, count, dest, row, col, order, ids):
    me = lax.axis_index("ra")

    def clear(slot, carry):
        order[slot] = 0
        ids[slot] = TILES
        return carry

    lax.fori_loop(0, owners * capacity, clear, 0)

    def zero(owner, carry):
        count[owner] = 0
        return carry

    lax.fori_loop(0, owners, zero, 0)

    def place(block, carry):
        owner = dest[block]
        rank = count[owner]
        count[owner] = rank + 1
        slot = (owner ^ me) * capacity + rank
        order[slot] = block
        ids[slot] = row[block] * (TC + 1) + col[block]
        return carry

    lax.fori_loop(0, dest.shape[0], place, 0)


def routed(tile, route):
    if route == "all":
        return tile
    border = lax.rem(tile, TC + 1) == TC
    if route == "inner":
        return lax.select(border, TILES, tile)
    return lax.select(border, tile - TC, TILES)


def blocks_body(capacity, pieces, order, ids, widx, arrays, outs, buffers, sem, meanwhile=None):
    taps, pixels, ivar, table = arrays
    px, iv, rt, ct = buffers
    side, wide = ivar.shape[1], pixels.shape[1]
    copies = []
    steps = sorted(set(step for step, _, _ in pieces), key=[p[0] for p in pieces].index)
    for index, step in enumerate(steps):
        for rank in range(capacity):
            at = index * capacity + rank
            block = order[step * capacity + rank]
            pairs = (
                (pixels.at[block], px.at[at]),
                (ivar.at[block], iv.at[at]),
                (table.at[widx[0, block]], rt.at[at]),
                (table.at[widx[1, block]], ct.at[at]),
            )
            for kind, (source, target) in enumerate(pairs):
                copy = pltpu.make_async_copy(source, target, sem.at[kind, at])
                copy.start()
                copies.append(copy)
    if meanwhile is not None:
        meanwhile()
    slots = [step * capacity + rank for step in steps for rank in range(capacity)]
    lines = tap_lines(taps, order, slots)
    for index, step in enumerate(steps):
        at = range(index * capacity, (index + 1) * capacity)
        for copy in copies[4 * at[0] : 4 * (at[-1] + 1)]:
            copy.wait()
        cols = [banded(lines[i : i + 1, 128:], side, wide) for i in at]
        rows = [banded(lines[i : i + 1, :128], side, wide) for i in at]
        passed = [dot_t(px[i], k).astype(jnp.bfloat16) for i, k in zip(at, cols)]
        weighted = [
            (dot(k, p) * iv[i].astype(jnp.float32)).astype(jnp.bfloat16)
            for i, k, p in zip(at, rows, passed)
        ]
        middle = [
            dot(rt[i], jnp.concatenate([w, iv[i]], 1)).astype(jnp.bfloat16)
            for i, w in zip(at, weighted)
        ]
        result = []
        for i, m in zip(at, middle):
            both = jnp.concatenate([m[:, :side], m[:, side:]], 0)
            result.append(dot_t(both, ct[i]).astype(jnp.bfloat16))
        which = lax.broadcasted_iota(jnp.int32, (IDS, side), 0)
        for (owner, ranks, route), out in zip(pieces, outs):
            if owner != step:
                continue
            tiles = jnp.full((IDS, side), TILES, jnp.int32)
            for place, rank in enumerate(ranks):
                out[pl.ds(place * 2 * side, 2 * side), :] = result[rank]
                tile = routed(ids[step * capacity + rank], route)
                tiles = jnp.where(which == place, tile, tiles)
            at_end = pl.ds(len(ranks) * 2 * side, IDS)
            out[at_end, :] = tiles.astype(jnp.float32).astype(jnp.bfloat16)


def first_kernel(owners, capacity, pieces, *refs):
    dest, row, col, widx = refs[:4]
    arrays, refs = refs[4:8], refs[8:]
    order, ids = refs[:2]
    outs, refs = refs[2 : 2 + len(pieces)], refs[2 + len(pieces) :]
    step = pieces[0][0]
    first = lax.axis_index("ra") ^ step

    base = step * capacity
    for rank in range(capacity):
        refs[-2][rank] = 0
    rank = jnp.int32(0)
    for block in range(dest.shape[0]):
        refs[-2][rank] = block
        rank = rank + (dest[block] == first).astype(jnp.int32)
    for place in range(capacity):
        order[base + place] = lax.select(place < rank, refs[-2][place], 0)
    fill = functools.partial(slots_body, owners, capacity, refs[-1], dest, row, col, order, ids)
    blocks_body(capacity, pieces, order, ids, widx, arrays, outs, refs[:4], refs[4], fill)


def next_kernel(capacity, pieces, *refs):
    order, ids, widx = refs[:3]
    arrays, refs = refs[3:7], refs[8:]
    outs, refs = refs[: len(pieces)], refs[len(pieces) :]
    blocks_body(capacity, pieces, order, ids, widx, arrays, outs, refs[:4], refs[4])


def fetched(sources, targets, sem):
    copies = []
    for index, (source, target) in enumerate(zip(sources, targets)):
        copy = pltpu.make_async_copy(source, target, sem.at[index])
        copy.start()
        copies.append(copy)
    return copies


def add_parcel(parcel, side, add):
    count = parcel.shape[0] // (2 * side)
    tiles = parcel[pl.ds(count * 2 * side, IDS), :].astype(jnp.float32)
    for rank in range(count):
        tile = tiles[rank : rank + 1]
        add(jnp.max(tile).astype(jnp.int32), parcel.at[pl.ds(rank * 2 * side, 2 * side), :])


def early_kernel(count, *refs):
    parcels, (total, *buffer, sem) = refs[:count], refs[count:]
    side = total.shape[2]
    copies = fetched(parcels, buffer, sem)
    total[...] = jnp.zeros_like(total)

    def add(tile, block):
        total[tile] = total[tile] + block[...].astype(jnp.float32)

    for index, copy in enumerate(copies):
        copy.wait()
        add_parcel(buffer[index], side, add)


def border_kernel(count, total, *refs):
    parcels, (border, sums, *buffer, sem) = refs[:count], refs[count:]
    side = border.shape[2]
    columns = [total.at[row * (TC + 1) + TC] for row in range(TR)]
    targets = [sums.at[row] for row in range(TR)] + buffer
    copies = fetched(columns + list(parcels), targets, sem)
    sums[TR] = jnp.zeros_like(sums[TR])
    for copy in copies:
        copy.wait()

    def add(tile, block):
        row = lax.select(lax.rem(tile, TC + 1) == TC, lax.div(tile, TC + 1), TR)
        sums[row] = sums[row] + block[...].astype(jnp.float32)

    for index in range(count):
        add_parcel(buffer[index], side, add)
    for row in range(TR):
        border[row] = sums[row].astype(jnp.bfloat16)


def inner_kernel(count, total, *refs):
    parcels, (coadd, weight_map, edge, sums, ratio, weight, *buffer, sem, out_sem) = (
        refs[:count],
        refs[count:],
    )
    side = edge.shape[2]
    for copy in fetched([total] + list(parcels), [sums] + buffer, sem):
        copy.wait()

    def add(tile, block):
        sums[tile] = sums[tile] + block[...].astype(jnp.float32)

    for index in range(count):
        add_parcel(buffer[index], side, add)
    copies = []
    for row in range(TR):
        pairs = [(sums.at[row * (TC + 1)], edge.at[row])]
        for col in range(TC):
            both = sums[row * (TC + 1) + col]
            num, den = both[:side], both[side:]
            at = pl.ds(col * side, side)
            weight[row, :, at] = den
            ratio[row, :, at] = num / jnp.maximum(den, 1.0)
        rows = pl.ds(row * side, side)
        pairs += [(ratio.at[row], coadd.at[rows]), (weight.at[row], weight_map.at[rows])]
        for kind, (source, target) in enumerate(pairs):
            copies.append(pltpu.make_async_copy(source, target, out_sem.at[kind, row]))
            copies[-1].start()
    for copy in copies:
        copy.wait()


def edge_kernel(edge, border, coadd_in, map_in, coadd, weight_map, sums, more, num, den, sem, in_sem):
    side = edge.shape[2]
    sources = [edge.at[row] for row in range(TR)] + [border.at[row] for row in range(TR)]
    targets = [sums.at[row] for row in range(TR)] + [more.at[row] for row in range(TR)]
    arriving = fetched(sources, targets, in_sem)
    copies = []
    for row in range(TR):
        arriving[row].wait()
        arriving[TR + row].wait()
        both = sums[row] + more[row].astype(jnp.float32)
        num[row] = both[:side] / jnp.maximum(both[side:], 1.0)
        den[row] = both[side:]
        for kind, (source, target) in enumerate(((num, coadd), (den, weight_map))):
            copy = pltpu.make_async_copy(
                source.at[row],
                target.at[pl.ds(row * side, side), pl.ds(0, side)],
                sem.at[kind, row],
            )
            copy.start()
            copies.append(copy)
    for copy in copies:
        copy.wait()


def exchanged(value, owners, step, beyond=0):
    if step == 0 and not beyond:
        return value
    pairs = [(source, ((source ^ step) + beyond) % owners) for source in range(owners)]
    return lax.ppermute(value, "ra", pairs)


def passed_along(value, owners):
    return lax.ppermute(value, "ra", [(source, (source + 1) % owners) for source in range(owners)])


def planned(owners):
    half = owners // 2
    far = list(range(half, owners))
    near = list(range(half - 1, -1, -1))
    over, side = near[: half // 2], near[half // 2 : -2]
    cut = len(over) * 3 // 4
    steps = far[:3] + over[:cut] + far[3:4] + over[cut:] + far[4:5] + side + far[5:] + near[-2:]
    groups = [steps[:1], steps[1:2], steps[2:4]]
    for start in range(4, owners, 4):
        groups.append(steps[start : start + 4])
    return groups, far[-1], over[len(over) - LATE_OVER :] + far[len(far) - LATE :]


def shards(pixels, inverse_var, psf_taps, warp_table, warp_index, dest_patch, tile_row, tile_col):
    blocks, wide = pixels.shape[:2]
    side = inverse_var.shape[1]
    owners = lax.axis_size("ra")
    capacity = max(2, blocks // owners)
    bf16, f32 = jnp.bfloat16, jnp.float32
    slots = jax.ShapeDtypeStruct((owners * capacity,), jnp.int32)
    totals = (TILES + 1, 2 * side, side)

    def cost(count, flops, moved):
        return pl.CostEstimate(flops=count * flops, bytes_accessed=count * moved, transcendentals=0)

    widx = warp_index.T
    arrays = (jnp.transpose(psf_taps, (2, 1, 0)), pixels, inverse_var, warp_table)
    groups, last, slow = planned(owners)

    def buffers(count):
        return [
            pltpu.VMEM((count, wide, wide), bf16),
            pltpu.VMEM((count, side, side), bf16),
            pltpu.VMEM((count, side, side), bf16),
            pltpu.VMEM((count, side, side), bf16),
            pltpu.SemaphoreType.DMA((4, count)),
        ]

    def parcel(count):
        return jax.ShapeDtypeStruct((count * 2 * side + IDS, side), bf16)

    everything, kept = tuple(range(capacity)), capacity - min(BYPASS, capacity - 1)
    final = everything[kept:]
    cut = [(last, everything[:kept], "all"), (last, final, "inner"), (last, final, "border")]
    sent = {}
    before = None
    for index, steps in enumerate(groups):
        count = len(steps) * capacity
        pieces = []
        for step in steps:
            pieces += cut if step == last else [(step, everything, "all")]
        parcels = [parcel(len(ranks)) for _, ranks, _ in pieces]
        shared = dict(
            scratch_shapes=buffers(count),
            cost_estimate=cost(count, 30 << 20, 1 << 18),
            compiler_params=WHOLE,
            name="blocks_" + str(index),
        )
        if index == 0:
            shared["scratch_shapes"] += [
                pltpu.SMEM((capacity + 1,), jnp.int32),
                pltpu.SMEM((owners,), jnp.int32),
            ]
            order, ids, *outs = pl.pallas_call(
                functools.partial(first_kernel, owners, capacity, pieces),
                out_shape=[slots, slots] + parcels,
                in_specs=[SMEM] * 4 + [VMEM] + [ANY] * 3,
                out_specs=[SMEM] * 2 + [VMEM] * len(parcels),
                **shared,
            )(dest_patch[:, 0], tile_row, tile_col, widx, *arrays)
        else:
            outs = pl.pallas_call(
                functools.partial(next_kernel, capacity, pieces),
                out_shape=parcels,
                in_specs=[SMEM] * 3 + [VMEM] + [ANY] * 4,
                out_specs=[VMEM] * len(parcels),
                **shared,
            )(order, ids, widx, *arrays, before)
        before = outs[0]
        sent.update({(step, route): out for (step, _, route), out in zip(pieces, outs)})
    steps = [step for group in groups for step in group]
    arrived = {}
    for step in steps:
        arrived[step] = exchanged(sent[step, "all"], owners, step)
    late = [arrived[step] for step in slow]
    early = [arrived[step] for step in steps if step not in slow]
    ending = []
    for route, beyond in (("inner", 0), ("border", 1)):
        ending.append(exchanged(sent[last, route], owners, last, beyond))

    def held(parcels, others):
        scratch = [pltpu.VMEM(value.shape, bf16) for value in parcels]
        return scratch + [pltpu.SemaphoreType.DMA((len(parcels) + others,))]

    total = pl.pallas_call(
        functools.partial(early_kernel, len(early)),
        out_shape=jax.ShapeDtypeStruct(totals, f32),
        in_specs=[ANY] * len(early),
        out_specs=VMEM,
        scratch_shapes=held(early, 0),
        cost_estimate=cost(len(early) * capacity, 1 << 16, 1 << 17),
        compiler_params=WHOLE,
        name="early_sum",
    )(*early)
    border = pl.pallas_call(
        functools.partial(border_kernel, len(late)),
        out_shape=jax.ShapeDtypeStruct((TR, 2 * side, side), bf16),
        in_specs=[ANY] * (1 + len(late)),
        out_specs=VMEM,
        scratch_shapes=[pltpu.VMEM((TR + 1, 2 * side, side), f32)] + held(late, TR),
        compiler_params=WHOLE,
        name="border_sum",
    )(total, *late)
    border = passed_along(border, owners)
    rest = late + ending
    sky = jax.ShapeDtypeStruct((TR * side, TC * side), f32)
    coadd, weight_map, edge = pl.pallas_call(
        functools.partial(inner_kernel, len(rest)),
        out_shape=[sky, sky, jax.ShapeDtypeStruct((TR, 2 * side, side), f32)],
        in_specs=[ANY] * (1 + len(rest)),
        out_specs=[ANY] * 3,
        scratch_shapes=[pltpu.VMEM(totals, f32)]
        + [pltpu.VMEM((TR, side, TC * side), f32)] * 2
        + held(rest, 1)
        + [pltpu.SemaphoreType.DMA((3, TR))],
        cost_estimate=cost(1, 1 << 22, 1 << 23),
        compiler_params=WHOLE,
        name="inner",
    )(total, *rest)
    return tuple(
        pl.pallas_call(
            edge_kernel,
            out_shape=[sky, sky],
            in_specs=[ANY] * 4,
            out_specs=[ANY] * 2,
            scratch_shapes=[
                pltpu.VMEM((TR, 2 * side, side), f32),
                pltpu.VMEM((TR, 2 * side, side), bf16),
                pltpu.VMEM((TR, side, side), f32),
                pltpu.VMEM((TR, side, side), f32),
                pltpu.SemaphoreType.DMA((2, TR)),
                pltpu.SemaphoreType.DMA((2 * TR,)),
            ],
            input_output_aliases={2: 0, 3: 1},
            compiler_params=WHOLE,
            name="edge",
        )(edge, border, coadd, weight_map)
    )


def solution(mesh):
    placed = (
        P(("grp", "ra"), None, None),
        P(("grp", "ra"), None, None),
        P(("grp", "ra"), None, None),
        P(),
        P(("grp", "ra"), None),
        P(("grp", "ra"), None),
        P(("grp", "ra")),
        P(("grp", "ra")),
    )
    return jax.shard_map(
        shards,
        mesh=mesh,
        in_specs=placed,
        out_specs=(P("grp", "ra"), P("grp", "ra")),
        check_vma=False,
    )
```
